512 devices in a mesh: gx: 64 (over z, x, core), ta: 8 (over y).
Axes of the slice: x: 4, y: 8, z: 8, core: 2. Of those that a mesh axis runs over, the one named last changes fastest.
Arguments:
- d_out: bfloat16 [16384, 4096], P('gx', 'ta'), may hold values from -0.75 to 0.75
- kept: int32 [2048], P('gx'), may hold values from 0 to 16383, as said below
- expert_ids: int32 [2048, 8], P('gx'), may hold values from 0 to 63, all different within a row; in each aligned block of 32 rows (0 to 31, 32 to 63, ...) at most 8 rows name the same one
- gates: bfloat16 [2048, 8], P('gx'), may hold values from 0.049804688 to 1
- down_weight: bfloat16 [64, 1536, 4096], P('gx', 'ta'), may hold values from -0.15625 to 0.15625
- gate_pre: bfloat16 [64, 1536, 512], P('gx', 'ta'), may hold values from -6 to 6
- up_pre: bfloat16 [64, 1536, 512], P('gx', 'ta'), may hold values from -6 to 6
- query: bfloat16 [2048, 8192], P('gx', 'ta'), may hold values from -6 to 6
- keys: bfloat16 [2048, 512], P('gx'), may hold values from -6 to 6
- values: bfloat16 [2048, 512], P('gx'), may hold values from -6 to 6
- d_attn: bfloat16 [2048, 8192], P('gx', 'ta'), may hold values from -12 to 12
Outputs:
- d_down: bfloat16 [64, 1536, 4096], P('gx', 'ta')
- d_gate_pre: bfloat16 [64, 1536, 512], P('gx', 'ta')
- d_up_pre: bfloat16 [64, 1536, 512], P('gx', 'ta')
- d_gates: float32 [2048, 8], P('gx')
- d_query: bfloat16 [2048, 8192], P('gx', 'ta')
- d_key: float32 [2048, 512], P('gx')
- d_value: float32 [2048, 512], P('gx')
The draws below stay inside these ranges and needn't reach their ends.
Inputs may be any that keep to these rules, and one draw needn't show every extreme that they name: `kept`: rising; the 32 selected tokens of block i lie in positions i * 256 to (i + 1) * 256 - 1 and include both ends. `expert_ids`: each row names 8 different experts; in each aligned block of 32 rows no expert is named more than 8 times.
All inputs are finite; a program needn't handle non-finite values.
Results may differ from the reference program's by a relative error of at most 0.0068.
Values may be sent and summed in bfloat16 or wider, within the bound.
No kernel may reach another device: no remote copies, remote signals or barrier semaphores. Data moves between devices by JAX's collectives and lax.ppermute only.
A program may use at most 64 MiB of HBM per device.

```python
import math
import jax
import jax.numpy as jnp
import numpy as np
from jax import lax

D = 4096
FF = 1536
H = 64
KVH = 4
HD = 128
TOPK = 8
KEEP_DEV = 32
TOK_DEV = 256
TOKENS = 16384
KEPT = 2048
EXPERTS = 64
CAP = 8
SLOTS = 512


def drawn_pattern(key):
    base = jax.random.normal(jax.random.fold_in(key, 31), (KEPT, KVH * HD), jnp.float32)
    return base


def draw_keys(key, part):
    base = drawn_pattern(key)
    result = jnp.clip(base, -4.0, 4.0)
    return result.astype(jnp.bfloat16)


def draw_query(key, part):
    result = jnp.clip(jax.random.normal(jax.random.fold_in(key, 34), (KEPT, H * HD), jnp.float32), -4.0, 4.0)
    return result.astype(jnp.bfloat16)


def draw_kept(key, part):
    blocks = KEPT // KEEP_DEV

    def one_block(index):
        inner = jax.random.permutation(jax.random.fold_in(key, index), TOK_DEV - 2)[:KEEP_DEV - 2] + 1
        chosen = jnp.sort(inner).astype(jnp.int32)
        whole = jnp.concatenate([jnp.zeros((1,), jnp.int32), chosen, jnp.full((1,), TOK_DEV - 1, jnp.int32)])
        return whole + index * TOK_DEV
    return jax.vmap(one_block)(jnp.arange(blocks, dtype=jnp.int32)).reshape(-1)


def block_scale(key, extent, cuts, smallest, largest):
    gain = 1.0
    for dim, shards_of in cuts:
        draws = jax.random.uniform(jax.random.fold_in(jax.random.fold_in(key, 6), dim), (shards_of,), jnp.float32, smallest / len(cuts), largest / len(cuts))
        gain = gain * jnp.repeat(jnp.exp(draws), extent[dim] // shards_of).reshape((-1,) + (1,) * (len(extent) - 1 - dim))
    return gain


def assign_block(own_key, own, number, rows, count, top, reach, lean):
    order = jax.random.permutation(own_key, count)
    heavy_load, usual = shares(count, rows * top, reach, lean, True), shares(count, rows * top, reach, lean, False)
    places = jnp.arange(count)

    def named(tallies, turn):
        used = int((tallies > 0).sum())
        fixed = max(1, used // 4)
        passed = fixed + (places - fixed + turn * (used - fixed)) % max(1, count - fixed)
        return jnp.zeros((count,), jnp.int32).at[order[jnp.where(places < fixed, places, passed)]].set(jnp.asarray(tallies, jnp.int32))

    tallies = jnp.where(number % 4 == 0, named(heavy_load, number // 4), named(usual, number - number // 4 - 1))
    mixed = jax.random.permutation(jax.random.fold_in(own, 3), count)
    source_of, sink = mixed[0:count // 2 * 2:2], mixed[1:count // 2 * 2:2]
    margin = jnp.minimum(tallies[source_of] - 1, reach - tallies[sink]) // 2
    margin = jnp.where((source_of == order[0]) | (sink == order[0]) | (tallies[sink] == 0), 0, jnp.maximum(margin, 0))
    passed = jax.random.randint(jax.random.fold_in(own, 4), (count // 2,), 0, 1 << 20) % (margin + 1)
    tallies = tallies.at[source_of].add(-passed).at[sink].add(passed)
    members = jnp.searchsorted(jnp.cumsum(tallies), jnp.arange(rows * top), side="right").astype(jnp.int32)
    listing = members.reshape(top, rows).T
    listing = listing[jax.random.permutation(jax.random.fold_in(own, 1), rows)]
    turn = jax.random.randint(jax.random.fold_in(own, 2), (rows, 1), 0, top)
    return jnp.take_along_axis(listing, (jnp.arange(top)[None, :] + turn) % top, axis=1)


def shares(count, total, limit, lean, full):
    loads = [(1 << 20) // math.isqrt(grade ** lean) + 1 for grade in range(1, count + 1)]
    largest = limit if full else min(limit, max(-(-total // count), total * loads[0] // sum(loads)))
    least = 1 if total - largest >= count - 1 else 0
    given, surplus = [largest] + [least] * (count - 1), total - largest - least * (count - 1)
    while surplus > 0:
        candidates = [i for i in range(1, count) if given[i] < largest] or [i for i in range(1, count) if given[i] < limit]
        mass, left = sum([loads[i] for i in candidates]), surplus
        for i in candidates:
            more = min(limit - given[i], max(1, left * loads[i] // mass), surplus)
            given[i] = given[i] + more
            surplus = surplus - more
    return np.array(given)


def noise(rng, dims, scale, bound, pieces=(), held_as=jnp.bfloat16):
    level = block_scale(rng, dims, pieces, -0.22, 0.18) if pieces else 1.0
    values = jax.random.normal(rng, dims, jnp.float32) * scale * level
    return jnp.minimum(jnp.maximum(values, -bound), bound).astype(held_as)


def setup_inputs(seed: int = 0) -> dict:
    key_of = jax.random.split(jax.random.key(seed), 12)
    d_out = noise(key_of[0], (TOKENS, D), 0.125, 0.75, ((0, 64), (1, 8)))
    kept = draw_kept(jax.random.fold_in(key_of[11], 71), 0)
    expert_ids_keys = jax.random.split(jax.random.fold_in(key_of[2], 1), KEPT // KEEP_DEV)
    expert_ids_turns = jax.random.permutation(jax.random.fold_in(key_of[2], 3), KEPT // KEEP_DEV)
    expert_ids = jax.vmap(lambda own, number: assign_block(jax.random.fold_in(key_of[2], 2), own, number, KEEP_DEV, EXPERTS, TOPK, CAP, 2))(expert_ids_keys, expert_ids_turns).reshape((KEPT, TOPK))
    gates = jnp.clip(jnp.exp(math.log(1.0) - 2.9996462 * jax.random.uniform(key_of[3], (KEPT, TOPK), jnp.float32) ** block_scale(key_of[3], (KEPT, TOPK), ((0, 64),), -0.2, 0.2)), 0.049804688, 1.0).astype(jnp.bfloat16)
    down_weight = noise(key_of[4], (EXPERTS, FF, D), FF ** -0.5, 0.15625, ((0, 64), (1, 8)))
    gate_pre = noise(key_of[5], (EXPERTS, FF, SLOTS), 1.0, 6.0, ((0, 64), (1, 8)))
    up_pre = noise(key_of[6], (EXPERTS, FF, SLOTS), 1.0, 6.0, ((0, 64), (1, 8)))
    query = draw_query(jax.random.fold_in(key_of[11], 71), 0)
    keys = draw_keys(jax.random.fold_in(key_of[11], 71), 0)
    values = noise(key_of[9], (KEPT, KVH * HD), 1.0, 6.0, ((0, 64),))
    d_attn = noise(key_of[10], (KEPT, H * HD), 2.0, 12.0, ((0, 64), (1, 8)))
    return {"d_out": d_out, "kept": kept, "expert_ids": expert_ids, "gates": gates, "down_weight": down_weight, "gate_pre": gate_pre, "up_pre": up_pre, "query": query, "keys": keys, "values": values, "d_attn": d_attn}


def expert_backward(parts):
    weight, gate_in, up_in, rows, slot_weight = parts
    z = lax.dot_general(weight, rows, (((1,), (1,)), ((), ())), preferred_element_type=jnp.float32)
    g = gate_in.astype(jnp.float32)
    u = up_in.astype(jnp.float32)
    sig = jax.nn.sigmoid(g)
    act = g * sig
    hidden = act * u
    slot_dots = jnp.sum(hidden * z, axis=0)
    grad_hidden = z * slot_weight[None, :]
    grad_up = (grad_hidden * act).astype(jnp.bfloat16)
    grad_gate = (grad_hidden * u * sig * (1.0 + g * (1.0 - sig))).astype(jnp.bfloat16)
    weighted = (hidden * slot_weight[None, :]).astype(jnp.bfloat16)
    grad_weight = jnp.dot(weighted, rows, preferred_element_type=jnp.float32).astype(jnp.bfloat16)
    return grad_weight, grad_gate, grad_up, slot_dots


def reference(d_out, kept, expert_ids, gates, down_weight, gate_pre, up_pre, query, keys, values, d_attn):
    picked = jnp.take(d_out, kept, axis=0)
    blocks = KEPT // KEEP_DEV
    ids_block = expert_ids.reshape(blocks, KEEP_DEV * TOPK)
    onehot = (ids_block[:, :, None] == jnp.arange(EXPERTS, dtype=jnp.int32)[None, None, :]).astype(jnp.int32)
    rank = jnp.sum((jnp.cumsum(onehot, axis=1) - onehot) * onehot, axis=2)
    slot = (jnp.arange(blocks, dtype=jnp.int32)[:, None] * CAP + rank).reshape(-1).astype(jnp.int32)
    flat_ids = expert_ids.reshape(-1).astype(jnp.int32)
    owner = jnp.arange(KEPT * TOPK, dtype=jnp.int32) // TOPK
    slot_rows = jnp.zeros((EXPERTS, SLOTS, D), jnp.bfloat16).at[flat_ids, slot].set(jnp.take(picked, owner, axis=0))
    slot_weight = jnp.zeros((EXPERTS, SLOTS), jnp.float32).at[flat_ids, slot].set(gates.reshape(-1).astype(jnp.float32))
    d_down, d_gate_pre, d_up_pre, slot_dots = lax.map(expert_backward, (down_weight, gate_pre, up_pre, slot_rows, slot_weight))
    d_gates = slot_dots[flat_ids, slot].reshape(KEPT, TOPK)

    scale = HD ** -0.5
    group = H // KVH
    query_heads = query.reshape(KEPT, H, HD)
    grad_heads = d_attn.reshape(KEPT, H, HD)
    causal = jnp.arange(KEPT)[:, None] >= jnp.arange(KEPT)[None, :]
    dq_parts = []
    dk_parts = []
    dv_parts = []
    for head_kv in range(KVH):
        key_head = keys[:, head_kv * HD:(head_kv + 1) * HD]
        value_head = values[:, head_kv * HD:(head_kv + 1) * HD]

        def one_head(parts):
            q_head, o_head = parts
            scores = jnp.dot(q_head, key_head.T, preferred_element_type=jnp.float32) * scale
            scores = jnp.where(causal, scores, -1e30)
            top = jnp.max(scores, axis=1, keepdims=True)
            expo = jnp.exp(scores - top)
            probs = expo / jnp.sum(expo, axis=1, keepdims=True)
            grad_probs = jnp.dot(o_head, value_head.T, preferred_element_type=jnp.float32)
            grad_scores = probs * (grad_probs - jnp.sum(probs * grad_probs, axis=1, keepdims=True))
            probs_b = probs.astype(jnp.bfloat16)
            grad_b = grad_scores.astype(jnp.bfloat16)
            dq_head = (jnp.dot(grad_b, key_head, preferred_element_type=jnp.float32) * scale).astype(jnp.bfloat16)
            dk_head = jnp.dot(grad_b.T, q_head, preferred_element_type=jnp.float32) * scale
            dv_head = jnp.dot(probs_b.T, o_head, preferred_element_type=jnp.float32)
            return dq_head, dk_head, dv_head

        heads_q = jnp.transpose(query_heads[:, head_kv * group:(head_kv + 1) * group], (1, 0, 2))
        heads_o = jnp.transpose(grad_heads[:, head_kv * group:(head_kv + 1) * group], (1, 0, 2))
        dq_head, dk_head, dv_head = lax.map(one_head, (heads_q, heads_o))
        dq_parts.append(dq_head)
        dk_parts.append(jnp.sum(dk_head, axis=0))
        dv_parts.append(jnp.sum(dv_head, axis=0))
    d_query = jnp.transpose(jnp.concatenate(dq_parts, axis=0), (1, 0, 2)).reshape(KEPT, H * HD)
    d_key = jnp.concatenate(dk_parts, axis=1)
    d_value = jnp.concatenate(dv_parts, axis=1)
    return d_down, d_gate_pre, d_up_pre, d_gates, d_query, d_key, d_value
```

```python
import jax
import jax.numpy as jnp
from jax import lax
from jax.sharding import Mesh, PartitionSpec as P

H = 64
KVH = 4
HD = 128
GX = ("z", "x", "c")
ZX = ("z", "x")


def exchange(values, axes):
    return lax.all_to_all(values, axes, split_axis=0, concat_axis=0, tiled=True)


def to_partner(values):
    return lax.ppermute(values, "c", [(0, 1), (1, 0)])


def slot_tables(expert_ids, gates, slots, cap):
    rows, top = expert_ids.shape
    lane = lax.broadcasted_iota(jnp.int32, (rows, slots), 1)
    expert = lane // cap
    named = jnp.zeros((rows, slots), jnp.float32)
    weight = jnp.zeros((rows, slots), jnp.float32)
    for j in range(top):
        hit = expert_ids[:, j : j + 1] == expert
        named = named + hit.astype(jnp.float32)
        weight = weight + jnp.where(hit, gates[:, j : j + 1].astype(jnp.float32), 0.0)
    below = lax.broadcasted_iota(jnp.int32, (rows, rows), 0) > lax.broadcasted_iota(
        jnp.int32, (rows, rows), 1
    )
    rank = jnp.dot(
        below.astype(jnp.bfloat16), named.astype(jnp.bfloat16), preferred_element_type=jnp.float32
    )
    taken = (named > 0.0) & (rank.astype(jnp.int32) == lane % cap)
    return taken, weight


def on_device(
    d_out, kept, expert_ids, gates, down_weight, gate_pre, up_pre, query, keys, values, d_attn
):
    core = lax.axis_index("c")
    chip = lax.axis_index(ZX)
    chips = lax.axis_size(ZX)
    n_experts = lax.axis_size(GX)
    n_ta = lax.axis_size("ta")
    keep_dev = kept.shape[0]
    tok_dev, width = d_out.shape
    top = expert_ids.shape[1]
    slots = gate_pre.shape[2]
    cap = slots // n_experts

    local_heads = query.shape[1] // HD
    group = H // KVH
    first_kv = lax.axis_index("ta") * local_heads // group
    kv = jnp.concatenate(
        [
            lax.dynamic_slice_in_dim(keys, first_kv * HD, HD, 1),
            lax.dynamic_slice_in_dim(values, first_kv * HD, HD, 1),
        ],
        axis=1,
    )

    at = kept % tok_dev
    pick = (at[:, None] == lax.broadcasted_iota(jnp.int32, (keep_dev, tok_dev), 1)).astype(
        jnp.bfloat16
    )
    picked = jnp.dot(pick, d_out, preferred_element_type=jnp.float32).astype(jnp.bfloat16)
    taken, weight_of = slot_tables(expert_ids, gates, slots, cap)
    taken_b = taken.astype(jnp.bfloat16)
    packed = lax.dot_general(
        taken_b, picked, (((0,), (0,)), ((), ())), preferred_element_type=jnp.float32
    ).astype(jnp.bfloat16)
    gate_row = jnp.sum(jnp.where(taken, weight_of, 0.0), axis=0).astype(jnp.bfloat16)
    message = jnp.concatenate(
        [packed, jnp.broadcast_to(gate_row[:, None], (slots, HD))], axis=1
    ).reshape(n_experts, cap, width + HD)
    arrived = exchange(message, GX).reshape(slots, width + HD)
    slot_weight = arrived[:, width].astype(jnp.float32)
    slot_rows = lax.all_gather(arrived[:, :width], "ta", axis=1, tiled=True)

    kv_own = exchange(jnp.broadcast_to(kv[None], (chips,) + kv.shape), ZX).reshape(-1, 2 * HD)
    kv_other = to_partner(kv_own)

    half = chips * keep_dev
    total = 2 * half
    kv_all = jnp.concatenate([kv_own, kv_other], axis=0)
    key_all = kv_all[:, :HD]
    value_all = kv_all[:, HD:]
    rows = keep_dev * local_heads
    query_rows = query.reshape(rows, HD)
    grad_rows = d_attn.reshape(rows, HD)
    scale = HD ** (-0.5)
    nt = (((1,), (1,)), ((), ()))
    tn = (((0,), (0,)), ((), ()))
    scores = lax.dot_general(query_rows, key_all, nt, preferred_element_type=jnp.float32) * scale
    column = lax.broadcasted_iota(jnp.int32, (rows, total), 1)
    at_core = jnp.where(column < half, core, 1 - core)
    inner = column % half
    key_pos = (inner // keep_dev * 2 + at_core) * keep_dev + inner % keep_dev
    query_pos = (chip * 2 + core) * keep_dev + lax.broadcasted_iota(
        jnp.int32, (rows, total), 0
    ) // local_heads
    scores = jnp.where(key_pos <= query_pos, scores, -1e30)
    top_score = jnp.max(scores, axis=1, keepdims=True)
    expo = jnp.exp(scores - top_score)
    probs = expo / jnp.sum(expo, axis=1, keepdims=True)
    grad_probs = lax.dot_general(grad_rows, value_all, nt, preferred_element_type=jnp.float32)
    grad_scores = probs * (grad_probs - jnp.sum(probs * grad_probs, axis=1, keepdims=True))
    probs_b = probs.astype(jnp.bfloat16)
    grad_b = grad_scores.astype(jnp.bfloat16)
    grad_query = jnp.dot(grad_b, key_all, preferred_element_type=jnp.float32) * scale
    grad_query = grad_query.astype(jnp.bfloat16).reshape(keep_dev, -1)
    key_part = lax.dot_general(grad_b, query_rows, tn, preferred_element_type=jnp.float32) * scale
    value_part = lax.dot_general(probs_b, grad_rows, tn, preferred_element_type=jnp.float32)
    part = jnp.concatenate([key_part, value_part], axis=1)
    from_other = to_partner(part[half:].astype(jnp.bfloat16))
    chip_part = (part[:half] + from_other.astype(jnp.float32)).astype(jnp.bfloat16)
    owned = jnp.sum(
        exchange(chip_part.reshape(chips, keep_dev, 2 * HD), ZX).astype(jnp.float32), axis=0
    )

    z = lax.dot_general(down_weight[0], slot_rows, nt, preferred_element_type=jnp.float32)
    g = gate_pre[0].astype(jnp.float32)
    u = up_pre[0].astype(jnp.float32)
    sig = jax.nn.sigmoid(g)
    act = g * sig
    hidden = act * u
    slot_dots = jnp.sum(hidden * z, axis=0)
    grad_hidden = z * slot_weight[None, :]
    grad_up = (grad_hidden * act).astype(jnp.bfloat16)[None]
    grad_gate = (grad_hidden * u * sig * (1.0 + g * (1.0 - sig))).astype(jnp.bfloat16)[None]
    weighted = (hidden * slot_weight[None, :]).astype(jnp.bfloat16)
    grad_weight = jnp.dot(weighted, slot_rows, preferred_element_type=jnp.float32).astype(
        jnp.bfloat16
    )[None]

    returned = exchange(slot_dots.reshape(n_experts, cap), GX).reshape(1, slots)
    mine = jnp.where(taken, returned, 0.0)
    expert = lax.broadcasted_iota(jnp.int32, (keep_dev, slots), 1) // cap
    gate_terms = jnp.concatenate(
        [
            jnp.sum(jnp.where(expert_ids[:, j : j + 1] == expert, mine, 0.0), axis=1, keepdims=True)
            for j in range(top)
        ],
        axis=1,
    )

    high = lax.reduce_precision(gate_terms, 8, 7)
    low = (gate_terms - high).astype(jnp.bfloat16)
    last = jnp.concatenate(
        [
            owned.astype(jnp.bfloat16),
            high.astype(jnp.bfloat16),
            low,
            jnp.zeros((keep_dev, HD - 2 * top), jnp.bfloat16),
        ],
        axis=1,
    )
    terms = exchange(jnp.broadcast_to(last[None], (n_ta,) + last.shape), "ta").astype(jnp.float32)
    gate_sum = jnp.sum(terms[:, :, 2 * HD : 2 * HD + 2 * top], axis=0)
    grad_gates = gate_sum[:, :top] + gate_sum[:, top:]
    heads = jnp.sum(
        terms[:, :, : 2 * HD].reshape(KVH, n_ta // KVH, keep_dev, 2 * HD), axis=1
    )
    grad_key = jnp.concatenate([heads[i, :, :HD] for i in range(KVH)], axis=1)
    grad_value = jnp.concatenate([heads[i, :, HD:] for i in range(KVH)], axis=1)
    return (grad_weight, grad_gate, grad_up, grad_gates, grad_query, grad_key, grad_value)


def solution(mesh):
    shape = dict(mesh.shape)
    fine = Mesh(mesh.devices.reshape(8, shape["gx"] // 16, 2, shape["ta"]), GX + ("ta",))
    in_specs = (
        P(GX, "ta"),
        P(GX),
        P(GX, None),
        P(GX, None),
        P(GX, "ta", None),
        P(GX, "ta", None),
        P(GX, "ta", None),
        P(GX, "ta"),
        P(GX, None),
        P(GX, None),
        P(GX, "ta"),
    )
    out_specs = (
        P(GX, "ta", None),
        P(GX, "ta", None),
        P(GX, "ta", None),
        P(GX, None),
        P(GX, "ta"),
        P(GX, None),
        P(GX, None),
    )
    return jax.shard_map(
        on_device, mesh=fine, in_specs=in_specs, out_specs=out_specs, check_vma=False
    )
```

```python
import functools

import jax
import jax.numpy as jnp
from jax import lax
from jax.experimental import pallas as pl
from jax.experimental.pallas import tpu as pltpu
from jax.sharding import Mesh, PartitionSpec as P


H = 64
KVH = 4
HD = 128
GX = ("z", "x", "c")
ZX = ("z", "x")
NT = (((1,), (1,)), ((), ()))
TN = (((0,), (0,)), ((), ()))
F32 = jnp.float32
BF16 = jnp.bfloat16


def exchange(values, axes):
    return lax.all_to_all(values, axes, split_axis=0, concat_axis=0, tiled=True)


def to_partner(values):
    return lax.ppermute(values, "c", [(0, 1), (1, 0)])


def along(values, step):
    n = lax.axis_size("ta")
    return lax.ppermute(values, "ta", [(i, (i + step) % n) for i in range(n)])


def iota(shape, dim):
    return lax.broadcasted_iota(jnp.int32, shape, dim)


def vmem():
    return pl.BlockSpec(memory_space=pltpu.VMEM)


def smem():
    return pl.BlockSpec(memory_space=pltpu.SMEM)


def call(body, outs, ins, cost):
    return pl.pallas_call(
        body,
        out_shape=outs,
        in_specs=[smem()] + [vmem()] * (len(ins) - 1),
        out_specs=jax.tree.map(lambda _: vmem(), outs),
        cost_estimate=pl.CostEstimate(flops=cost, bytes_accessed=cost // 100, transcendentals=0),
    )(*ins)


def pack_body(where, kept, ids, gates, d_out, keys, values, message, ranks):
    rows, top = ids.shape
    slots = message.shape[0]
    tok_dev, width = d_out.shape
    cap = 8
    head = pl.multiple_of(where[0] * HD, HD)
    lane = iota((rows, slots), 1)
    expert = lane // cap
    named = jnp.zeros((rows, slots), F32)
    weight = jnp.zeros((rows, slots), F32)
    for j in range(top):
        hit = ids[:, j : j + 1] == expert
        named = jnp.where(hit, 1.0, named)
        weight = jnp.where(hit, gates[:, j : j + 1].astype(F32), weight)
    below = (iota((rows, rows), 0) > iota((rows, rows), 1)).astype(F32).astype(BF16)
    rank = jnp.dot(below, named.astype(BF16), preferred_element_type=F32)
    place = (lane % cap).astype(F32)
    taken = jnp.where((named > 0.0) & (rank == place), 1.0, 0.0)
    pick = jnp.where(kept[...] % tok_dev == iota((rows, tok_dev), 1), 1.0, 0.0).astype(BF16)
    picked = jnp.dot(pick, d_out[...], preferred_element_type=F32).astype(BF16)
    message[:, :width] = lax.dot_general(
        taken.astype(BF16), picked, TN, preferred_element_type=F32
    ).astype(BF16)
    kv = jnp.concatenate([keys[:, pl.ds(head, HD)], values[:, pl.ds(head, HD)]], axis=1)
    kv = kv.astype(F32)
    pair = jnp.concatenate(
        [
            jnp.concatenate([kv[0:8], kv[16:24]], axis=0),
            jnp.concatenate([kv[8:16], kv[24:32]], axis=0),
        ],
        axis=1,
    ).astype(BF16)
    message[:, width : width + 4 * HD] = jnp.broadcast_to(
        pair[None], (slots // 16, 16, 4 * HD)
    ).reshape(slots, 4 * HD)
    message[:, width + 4 * HD :] = lax.dot_general(
        (taken * weight).astype(BF16), jnp.ones((rows, HD), BF16), TN, preferred_element_type=F32
    ).astype(BF16)
    found = jnp.zeros((rows, top), F32)
    for j in range(top):
        mine = jnp.where((ids[:, j : j + 1] == expert) & (taken > 0.0), place, 0.0)
        found = jnp.where(
            iota((rows, top), 1) == j, jnp.sum(mine, axis=1, keepdims=True), found
        )
    ranks[...] = found.astype(jnp.int32)


def attention_body(where, query, grad, mine, other, d_query, keep, send):
    core, block = where[0], where[1]
    keep_dev = query.shape[0]
    heads = query.shape[1] // HD
    rows = keep_dev * heads
    half = mine.shape[0]
    scale = HD ** (-0.5)

    def stacked(ref):
        return jnp.concatenate([ref[:, g * HD : (g + 1) * HD] for g in range(heads)], axis=0)

    q = stacked(query)
    o = stacked(grad)
    pieces = []
    query_pos = block * keep_dev + iota((rows, half), 0) % keep_dev
    row = iota((rows, half), 1)
    key_base = row // 8 * keep_dev + row % 8
    for ref, owner in ((mine, core), (other, 1 - core)):
        for q8 in range(2):
            key = ref[:, q8 * 2 * HD : q8 * 2 * HD + HD]
            value = ref[:, q8 * 2 * HD + HD : q8 * 2 * HD + 2 * HD]
            s = lax.dot_general(q, key, NT, preferred_element_type=F32) * scale
            s = jnp.where(key_base + (owner * 16 + q8 * 8) <= query_pos, s, -1e30)
            pieces.append((key, value, s, owner * 2 + q8))
    top = functools.reduce(
        jnp.maximum, [jnp.max(s, axis=1, keepdims=True) for _, _, s, _ in pieces]
    )
    expo = [jnp.exp(s - top) for _, _, s, _ in pieces]
    total = sum(jnp.sum(e, axis=1, keepdims=True) for e in expo)
    inv = 1.0 / total
    probs = [e * inv for e in expo]
    dps = [
        lax.dot_general(o, value, NT, preferred_element_type=F32) for _, value, _, _ in pieces
    ]
    mean = sum(jnp.sum(p * dp, axis=1, keepdims=True) for p, dp in zip(probs, dps))
    dq = jnp.zeros((rows, HD), F32)
    for (key, _, _, at), p, dp in zip(pieces, probs, dps):
        ds = (p * (dp - mean)).astype(BF16)
        dq = dq + jnp.dot(ds, key, preferred_element_type=F32)
        dk = lax.dot_general(ds, q, TN, preferred_element_type=F32) * scale
        dv = lax.dot_general(p.astype(BF16), o, TN, preferred_element_type=F32)
        for which, part in ((0, dk), (1, dv)):
            split = part.reshape(half // 16, 2, 8, HD)
            own = jnp.where(core == 0, split[:, 0], split[:, 1]).reshape(half // 2, HD)
            rest = jnp.where(core == 0, split[:, 1], split[:, 0]).reshape(half // 2, HD)
            lanes = pl.ds(pl.multiple_of(at * 2 * HD + which * HD, HD), HD)
            keep[:, lanes] = own
            send[:, lanes] = rest.astype(BF16)
    dq = (dq * scale).astype(BF16)
    for g in range(heads):
        d_query[:, g * HD : (g + 1) * HD] = dq[g * keep_dev : (g + 1) * keep_dev]


def shard_list(refs):
    own, r1, r2, r3, l1, l2, l3, r4, l4 = refs
    return ((0, own), (7, r1), (1, l1), (6, r2), (2, l2), (5, r3), (3, l3)), (r4, l4)


def expert_body(where, weight, gate_pre, up_pre, slot_gate, *refs):
    shards, last = shard_list(refs[:9])
    d_gate, d_up, weighted, dots = refs[9:]
    me = where[0]
    width = refs[0].shape[1]
    n = weight.shape[1] // width
    slots = refs[0].shape[0]

    def block(k):
        return weight[:, pl.ds(pl.multiple_of(lax.rem(me + k, n) * width, width), width)]

    z = jnp.zeros((weight.shape[0], slots), F32)
    for k, ref in shards:
        z = z + lax.dot_general(block(k), ref[...], NT, preferred_element_type=F32)
    z = z + jnp.concatenate(
        [lax.dot_general(block(4), ref[...], NT, preferred_element_type=F32) for ref in last],
        axis=1,
    )
    g = gate_pre[...].astype(F32)
    u = up_pre[...].astype(F32)
    sig = 1.0 / (1.0 + jnp.exp(-g))
    act = g * sig
    hidden = act * u
    dots[...] = jnp.sum(hidden * z, axis=0, keepdims=True)
    one = jnp.where(iota((8, HD), 1) == 0, 1.0, 0.0).astype(BF16)
    scale = lax.dot_general(one, slot_gate[...], NT, preferred_element_type=F32)[0:1]
    grad_hidden = z * scale
    d_up[...] = (grad_hidden * act).astype(BF16)
    d_gate[...] = (grad_hidden * u * sig * (1.0 + g * (1.0 - sig))).astype(BF16)
    weighted[...] = (hidden * scale).astype(BF16)


def down_body(where, weighted, *refs):
    shards, last = shard_list(refs[:9])
    out = refs[9]
    me = where[0]
    width = refs[0].shape[1]
    n = out.shape[1] // width
    w = weighted[...]

    def place(k):
        return pl.ds(pl.multiple_of(lax.rem(me + k, n) * width, width), width)

    for k, ref in shards:
        out[:, place(k)] = jnp.dot(w, ref[...], preferred_element_type=F32).astype(BF16)
    half = last[0].shape[0]
    out[:, place(4)] = (
        jnp.dot(w[:, :half], last[0][...], preferred_element_type=F32)
        + jnp.dot(w[:, half:], last[1][...], preferred_element_type=F32)
    ).astype(BF16)


def middle_body(where, terms, out):
    experts = out.shape[0]
    total = jnp.sum(terms[...], axis=0)
    slots = total.shape[1]
    cap = slots // experts
    spread = jnp.where(
        iota((experts, slots), 1) // cap == iota((experts, slots), 0), total, 0.0
    )
    lanes = jnp.where(iota((slots, HD), 0) % cap == iota((slots, HD), 1), 1.0, 0.0)
    out[...] = jnp.dot(
        spread, lanes, preferred_element_type=F32, precision=lax.Precision.HIGHEST
    )[:, None, :]


def gates_body(where, ids, ranks, returned, out):
    rows, top = ids.shape
    experts = returned.shape[0]
    pick = jnp.concatenate(
        [
            jnp.where(ids[:, j : j + 1] == iota((rows, experts), 1), 1.0, 0.0)
            for j in range(top)
        ],
        axis=0,
    )
    found = jnp.dot(
        pick,
        returned[...].reshape(experts, HD),
        preferred_element_type=F32,
        precision=lax.Precision.HIGHEST,
    )
    result = jnp.zeros((rows, top), F32)
    for j in range(top):
        hit = jnp.where(
            iota((rows, HD), 1) == ranks[:, j : j + 1], found[j * rows : (j + 1) * rows], 0.0
        )
        result = jnp.where(iota((rows, top), 1) == j, jnp.sum(hit, axis=1, keepdims=True), result)
    out[...] = result


def heads_body(where, terms, d_key, d_value):
    n = terms.shape[0]
    per = n // KVH
    for h in range(KVH):
        both = sum(terms[h * per + i].astype(F32) for i in range(per))
        for p in range(4):
            tokens = slice(p * 8, (p + 1) * 8)
            d_key[tokens, h * HD : (h + 1) * HD] = both[:, p * 2 * HD : p * 2 * HD + HD]
            d_value[tokens, h * HD : (h + 1) * HD] = both[:, p * 2 * HD + HD : (p + 1) * 2 * HD]


def on_device(
    d_out, kept, expert_ids, gates, down_weight, gate_pre, up_pre, query, keys, values, d_attn
):
    core = lax.axis_index("c")
    chips = lax.axis_size(ZX)
    me = lax.axis_index("ta")
    n_experts = lax.axis_size(GX)
    n_ta = lax.axis_size("ta")
    keep_dev = kept.shape[0]
    width = d_out.shape[1]
    top = expert_ids.shape[1]
    slots = gate_pre.shape[2]
    cap = slots // n_experts
    hidden = gate_pre.shape[1]
    struct = jax.ShapeDtypeStruct

    local_heads = query.shape[1] // HD
    first_kv = (me * local_heads // (H // KVH)).astype(jnp.int32).reshape(1)
    message, ranks = call(
        pack_body,
        (struct((slots, width + 5 * HD), BF16), struct((keep_dev, top), jnp.int32)),
        (first_kv, kept.reshape(keep_dev, 1), expert_ids, gates, d_out, keys, values),
        200_000_000,
    )
    arrived = exchange(message.reshape(n_experts, cap, -1), GX).reshape(slots, -1)
    own = arrived[:, :width]
    kv_mine = arrived[:, width : width + 4 * HD]
    slot_gate = arrived[:, width + 4 * HD :]

    r1, l1 = along(own, 1), along(own, -1)
    kv_other = to_partner(kv_mine)
    where = jnp.stack([core, lax.axis_index(GX)]).astype(jnp.int32)
    d_query, keep, send = call(
        attention_body,
        (
            struct((keep_dev, local_heads * HD), BF16),
            struct((slots // 2, 8 * HD), F32),
            struct((slots // 2, 8 * HD), BF16),
        ),
        (where, query, d_attn, kv_mine, kv_other),
        4_000_000_000,
    )
    r1, l1, send = lax.optimization_barrier((r1, l1, send))
    r2, l2 = along(r1, 1), along(l1, -1)
    chip_part = (keep + to_partner(send).astype(F32)).astype(BF16)
    summed = exchange(chip_part.reshape(chips, cap, 8 * HD), ZX)
    r3, l3 = along(r2, 1), along(l2, -1)
    r4, l4 = along(r3[: slots // 2], 1), along(l3[slots // 2 :], -1)
    shards = (own, r1, r2, r3, l1, l2, l3, r4, l4)
    owned = jnp.sum(summed.astype(F32), axis=0).astype(BF16)
    copies = exchange(jnp.broadcast_to(owned[None], (n_ta,) + owned.shape), "ta")
    d_key, d_value = call(
        heads_body,
        (struct((keep_dev, KVH * HD), F32), struct((keep_dev, KVH * HD), F32)),
        (where, copies),
        1_000_000,
    )

    at = me.astype(jnp.int32).reshape(1)
    d_gate, d_up, weighted, dots = call(
        expert_body,
        (
            struct((hidden, slots), BF16),
            struct((hidden, slots), BF16),
            struct((hidden, slots), BF16),
            struct((1, slots), F32),
        ),
        (at, down_weight[0], gate_pre[0], up_pre[0], slot_gate) + shards,
        3_000_000_000,
    )
    d_down = call(
        down_body, struct(down_weight.shape[1:], BF16), (at, weighted) + shards, 3_000_000_000
    )
    terms = exchange(jnp.broadcast_to(dots[None], (n_ta, 1, slots)), "ta")
    sums = call(middle_body, struct((n_experts, 1, HD), F32), (at, terms), 1_000_000)
    returned = exchange(sums, GX)
    d_gates = call(
        gates_body, struct((keep_dev, top), F32), (at, expert_ids, ranks, returned), 1_000_000
    )
    return (d_down[None], d_gate[None], d_up[None], d_gates, d_query, d_key, d_value)


def solution(mesh):
    shape = dict(mesh.shape)
    fine = Mesh(mesh.devices.reshape(8, shape["gx"] // 16, 2, shape["ta"]), GX + ("ta",))
    in_specs = (
        P(GX, "ta"),
        P(GX),
        P(GX, None),
        P(GX, None),
        P(GX, "ta", None),
        P(GX, "ta", None),
        P(GX, "ta", None),
        P(GX, "ta"),
        P(GX, None),
        P(GX, None),
        P(GX, "ta"),
    )
    out_specs = (
        P(GX, "ta", None),
        P(GX, "ta", None),
        P(GX, "ta", None),
        P(GX, None),
        P(GX, "ta"),
        P(GX, None),
        P(GX, None),
    )
    return jax.shard_map(
        on_device, mesh=fine, in_specs=in_specs, out_specs=out_specs, check_vma=False
    )
```

```python
import jax
import jax.numpy as jnp
from jax import lax
from jax.experimental import pallas as pl
from jax.experimental.pallas import tpu as pltpu
from jax.sharding import Mesh, PartitionSpec as P

H = 64
KVH = 4
HD = 128
GX = ("z", "x", "c")
ZX = ("z", "x")
NT = (((1,), (1,)), ((), ()))
TN = (((0,), (0,)), ((), ()))
F32 = jnp.float32
BF16 = jnp.bfloat16


def exchange(values, axes):
    return lax.all_to_all(values, axes, split_axis=0, concat_axis=0, tiled=True)


def to_partner(values):
    return lax.ppermute(values, "c", [(0, 1), (1, 0)])


def iota(shape, dim):
    return lax.broadcasted_iota(jnp.int32, shape, dim)


def call(body, outs, ins, flops, size, name):
    vmem = pl.BlockSpec(memory_space=pltpu.VMEM)
    return pl.pallas_call(
        body,
        out_shape=outs,
        in_specs=[pl.BlockSpec(memory_space=pltpu.SMEM)] + [vmem] * (len(ins) - 1),
        out_specs=jax.tree.map(lambda _: vmem, outs),
        cost_estimate=pl.CostEstimate(flops=flops, bytes_accessed=size, transcendentals=0),
        name=name,
    )(*ins)


def pack_body(where, kept, ids, gates, d_out, keys, values, message, kv, ranks):
    top, rows = ids.shape
    slots = message.shape[0]
    tok_dev, width = d_out.shape
    chips = kv.shape[0] // rows
    cap = 8
    head = pl.multiple_of(where[0] * HD, HD)
    slot = iota((slots, rows), 0)
    expert = slot // cap
    place = (slot % cap).astype(F32)
    named = jnp.zeros((slots, rows), F32)
    weight = jnp.zeros((slots, rows), F32)
    for j in range(top):
        hit = ids[j : j + 1, :] == expert
        named = jnp.where(hit, 1.0, named)
        weight = jnp.where(hit, gates[j : j + 1, :].astype(F32), weight)
    before = jnp.where(iota((rows, rows), 0) < iota((rows, rows), 1), 1.0, 0.0).astype(BF16)
    rank = jnp.dot(named.astype(BF16), before, preferred_element_type=F32)
    taken = jnp.where((named > 0.0) & (rank == place), 1.0, 0.0)
    pick = jnp.where(kept[...] % tok_dev == iota((tok_dev, rows), 0), 1.0, 0.0).astype(BF16)
    picked = lax.dot_general(pick, d_out[...], TN, preferred_element_type=F32).astype(BF16)
    message[:, :width] = jnp.dot(
        taken.astype(BF16), picked, preferred_element_type=F32
    ).astype(BF16)
    message[:, width:] = jnp.dot(
        (taken * weight).astype(BF16), jnp.ones((rows, HD), BF16), preferred_element_type=F32
    ).astype(BF16)
    for at, source in ((0, keys), (HD, values)):
        kv[:, at : at + HD] = jnp.broadcast_to(
            source[:, pl.ds(head, HD)][None], (chips, rows, HD)
        ).reshape(chips * rows, HD)
    for j in range(top):
        mine = jnp.where((ids[j : j + 1, :] == expert) & (taken > 0.0), place, 0.0)
        ranks[j : j + 1, :] = jnp.sum(mine, axis=0, keepdims=True).astype(jnp.int32)


def attention_body(where, query, grad, mine, other, d_query, keep, send):
    core, block = where[0], where[1]
    keep_dev = query.shape[0]
    heads = query.shape[1] // HD
    rows = keep_dev * heads
    half = mine.shape[0]
    scale = HD ** (-0.5)

    def stacked(ref):
        return jnp.concatenate([ref[:, g * HD : (g + 1) * HD] for g in range(heads)], axis=0)

    q = stacked(query)
    o = stacked(grad)
    query_pos = block * keep_dev + iota((rows, half), 0) % keep_dev
    column = iota((rows, half), 1)
    base = column // keep_dev * (2 * keep_dev) + column % keep_dev
    scores = []
    for ref, owner in ((mine, core), (other, 1 - core)):
        s = lax.dot_general(q, ref[:, :HD], NT, preferred_element_type=F32) * scale
        scores.append(jnp.where(base + owner * keep_dev <= query_pos, s, -1e30))
    top = jnp.maximum(*[jnp.max(s, axis=1, keepdims=True) for s in scores])
    expo = [jnp.exp(s - top) for s in scores]
    inv = 1.0 / sum(jnp.sum(e, axis=1, keepdims=True) for e in expo)
    probs = [e * inv for e in expo]
    dps = [
        lax.dot_general(o, ref[:, HD:], NT, preferred_element_type=F32) for ref in (mine, other)
    ]
    mean = sum(jnp.sum(p * dp, axis=1, keepdims=True) for p, dp in zip(probs, dps))
    dq = jnp.zeros((rows, HD), F32)
    for ref, p, dp, out in zip((other, mine), probs[::-1], dps[::-1], (send, keep)):
        ds = (p * (dp - mean)).astype(BF16)
        dk = lax.dot_general(ds, q, TN, preferred_element_type=F32) * scale
        dv = lax.dot_general(p.astype(BF16), o, TN, preferred_element_type=F32)
        out[:, :HD] = dk.astype(BF16)
        out[:, HD:] = dv.astype(BF16)
        dq = dq + jnp.dot(ds, ref[:, :HD], preferred_element_type=F32)
    dq = (dq * scale).astype(BF16)
    for g in range(heads):
        d_query[:, g * HD : (g + 1) * HD] = dq[g * keep_dev : (g + 1) * keep_dev]


def expert_body(weight, rows, gate_pre, up_pre, slot_gate, d_gate, d_up, weighted, dots, acc):
    step = pl.program_id(0)
    part = lax.dot_general(weight[...], rows[...], NT, preferred_element_type=F32)

    @pl.when(step == 0)
    def _():
        acc[...] = part

    @pl.when(step > 0)
    def _():
        acc[...] += part

    @pl.when(step == pl.num_programs(0) - 1)
    def _():
        z = acc[...]
        g = gate_pre[...].astype(F32)
        u = up_pre[...].astype(F32)
        sig = 1.0 / (1.0 + jnp.exp(-g))
        act = g * sig
        hidden = act * u
        dots[...] = jnp.sum(hidden * z, axis=0, keepdims=True)
        one = jnp.where(iota((8, HD), 1) == 0, 1.0, 0.0).astype(BF16)
        scale = lax.dot_general(one, slot_gate[...], NT, preferred_element_type=F32)[0:1]
        grad_hidden = z * scale
        d_up[...] = (grad_hidden * act).astype(BF16)
        d_gate[...] = (grad_hidden * u * sig * (1.0 + g * (1.0 - sig))).astype(BF16)
        weighted[...] = (hidden * scale).astype(BF16)


def down_body(weighted, rows, out):
    out[...] = jnp.dot(weighted[...], rows[...], preferred_element_type=F32).astype(BF16)


def merge_body(where, owned, dots, out):
    copies, rows, lanes = out.shape
    keep_dev = owned.shape[0]
    value = dots[...]
    high = value.astype(BF16)
    rest = value - high.astype(F32)
    middle = rest.astype(BF16)
    low = (rest - middle.astype(F32)).astype(BF16)
    row = iota((rows - keep_dev, lanes), 0)
    tail = jnp.zeros((rows - keep_dev, lanes), F32)
    for i, part in enumerate((high, middle, low)):
        for j in range(2):
            piece = part[:, j * lanes : (j + 1) * lanes].astype(F32)
            tail = jnp.where(row == 2 * i + j, piece, tail)
    for i in range(copies):
        out[i, :keep_dev] = owned[...]
        out[i, keep_dev:] = tail.astype(BF16)


def middle_body(where, terms, out):
    keep_dev = terms.shape[1] - 8
    lanes = terms.shape[2]
    total = jnp.sum(terms[:, keep_dev:, :].astype(F32), axis=0)
    half = out.shape[0] // 2
    cap = lanes // half
    spread = jnp.concatenate(
        [
            jnp.where(
                iota((half, lanes), 1) // cap == iota((half, lanes), 0),
                total[j : j + 1] + total[2 + j : 3 + j] + total[4 + j : 5 + j],
                0.0,
            )
            for j in range(2)
        ],
        axis=0,
    )
    place = jnp.where(iota((lanes, HD), 0) % cap == iota((lanes, HD), 1), 1.0, 0.0)
    out[...] = jnp.dot(
        spread, place, preferred_element_type=F32, precision=lax.Precision.HIGHEST
    )[:, None, :]


def gates_body(where, ids, ranks, returned, out):
    top, rows = ids.shape
    experts = returned.shape[0]
    table = returned[...].reshape(experts, HD)
    for j in range(top):
        pick = jnp.where(ids[j : j + 1, :] == iota((experts, rows), 0), 1.0, 0.0)
        found = lax.dot_general(
            table, pick, TN, preferred_element_type=F32, precision=lax.Precision.HIGHEST
        )
        hit = jnp.where(iota((HD, rows), 0) == ranks[j : j + 1, :], found, 0.0)
        out[j : j + 1, :] = jnp.sum(hit, axis=0, keepdims=True)


def heads_body(where, terms, d_key, d_value):
    keep_dev = d_key.shape[0]
    per = terms.shape[0] // KVH
    for h in range(KVH):
        both = sum(terms[h * per + i, :keep_dev].astype(F32) for i in range(per))
        d_key[:, h * HD : (h + 1) * HD] = both[:, :HD]
        d_value[:, h * HD : (h + 1) * HD] = both[:, HD:]


def on_device(
    d_out, kept, expert_ids, gates, down_weight, gate_pre, up_pre, query, keys, values, d_attn
):
    core = lax.axis_index("c")
    chips = lax.axis_size(ZX)
    me = lax.axis_index("ta")
    n_experts = lax.axis_size(GX)
    n_ta = lax.axis_size("ta")
    keep_dev = kept.shape[0]
    width = d_out.shape[1]
    top = expert_ids.shape[1]
    slots = gate_pre.shape[2]
    cap = slots // n_experts
    hidden = gate_pre.shape[1]
    struct = jax.ShapeDtypeStruct
    ids = expert_ids.T

    local_heads = query.shape[1] // HD
    first_kv = (me * local_heads // (H // KVH)).astype(jnp.int32)
    where = jnp.stack([first_kv, core.astype(jnp.int32), lax.axis_index(GX).astype(jnp.int32)])
    message, kv, ranks = call(
        pack_body,
        (
            struct((slots, width + HD), BF16),
            struct((chips * keep_dev, 2 * HD), BF16),
            struct((top, keep_dev), jnp.int32),
        ),
        (where, kept.reshape(1, keep_dev), ids, gates.T, d_out, keys, values),
        200_000_000,
        3_000_000,
        "pack",
    )
    arrived = exchange(message.reshape(n_experts, cap, -1), GX).reshape(slots, -1)
    slot_rows = lax.all_gather(arrived[:, :width], "ta", axis=1, tiled=True)
    slot_gate = arrived[:, width:]

    kv_mine = exchange(kv.reshape(chips, keep_dev, 2 * HD), ZX).reshape(-1, 2 * HD)
    kv_other = to_partner(kv_mine)
    half = chips * keep_dev
    d_query, keep, send = call(
        attention_body,
        (
            struct((keep_dev, local_heads * HD), BF16),
            struct((half, 2 * HD), BF16),
            struct((half, 2 * HD), BF16),
        ),
        (where[1:], query, d_attn, kv_mine, kv_other),
        1_000_000_000,
        4_000_000,
        "attention",
    )
    chip_part = (keep.astype(F32) + to_partner(send).astype(F32)).astype(BF16)
    summed = exchange(chip_part.reshape(chips, keep_dev, 2 * HD), ZX)
    owned = jnp.sum(summed.astype(F32), axis=0).astype(BF16)

    steps = n_ta
    whole = pl.BlockSpec((hidden, slots), lambda i: (0, 0))
    d_gate, d_up, weighted, dots = pl.pallas_call(
        expert_body,
        grid=(steps,),
        in_specs=[
            pl.BlockSpec((hidden, width), lambda i: (0, i)),
            pl.BlockSpec((slots, width), lambda i: (0, i)),
            whole,
            whole,
            pl.BlockSpec((slots, HD), lambda i: (0, 0)),
        ],
        out_specs=[whole, whole, whole, pl.BlockSpec((1, slots), lambda i: (0, 0))],
        out_shape=[struct((hidden, slots), BF16)] * 3 + [struct((1, slots), F32)],
        scratch_shapes=[pltpu.VMEM((hidden, slots), F32)],
        cost_estimate=pl.CostEstimate(
            flops=1_000_000_000, bytes_accessed=7_000_000, transcendentals=0
        ),
        name="expert",
    )(down_weight[0], slot_rows, gate_pre[0], up_pre[0], slot_gate)
    d_down = pl.pallas_call(
        down_body,
        grid=(steps,),
        in_specs=[whole, pl.BlockSpec((slots, width), lambda i: (0, i))],
        out_specs=pl.BlockSpec((hidden, width), lambda i: (0, i)),
        out_shape=struct(down_weight.shape[1:], BF16),
        cost_estimate=pl.CostEstimate(
            flops=1_000_000_000, bytes_accessed=6_000_000, transcendentals=0
        ),
        name="down",
    )(weighted, slot_rows)
    merged = call(
        merge_body,
        struct((n_ta, keep_dev + 8, 2 * HD), BF16),
        (where, owned, dots),
        1_000_000,
        200_000,
        "merge",
    )
    terms = exchange(merged, "ta")
    sums = call(
        middle_body, struct((n_experts, 1, HD), F32), (where, terms), 1_000_000, 100_000, "middle"
    )
    returned = exchange(sums, GX)
    d_gates = call(
        gates_body,
        struct((top, keep_dev), F32),
        (where, ids, ranks, returned),
        1_000_000,
        100_000,
        "gates",
    ).T
    d_key, d_value = call(
        heads_body,
        (struct((keep_dev, KVH * HD), F32), struct((keep_dev, KVH * HD), F32)),
        (where, terms),
        1_000_000,
        1_000_000,
        "heads",
    )
    return (d_down[None], d_gate[None], d_up[None], d_gates, d_query, d_key, d_value)


def solution(mesh):
    shape = dict(mesh.shape)
    fine = Mesh(mesh.devices.reshape(8, shape["gx"] // 16, 2, shape["ta"]), GX + ("ta",))
    in_specs = (
        P(GX, "ta"),
        P(GX),
        P(GX, None),
        P(GX, None),
        P(GX, "ta", None),
        P(GX, "ta", None),
        P(GX, "ta", None),
        P(GX, "ta"),
        P(GX, None),
        P(GX, None),
        P(GX, "ta"),
    )
    out_specs = (
        P(GX, "ta", None),
        P(GX, "ta", None),
        P(GX, "ta", None),
        P(GX, None),
        P(GX, "ta"),
        P(GX, None),
        P(GX, None),
    )
    return jax.shard_map(
        on_device, mesh=fine, in_specs=in_specs, out_specs=out_specs, check_vma=False
    )
```

```python
import jax
import jax.numpy as jnp
from jax import lax
from jax.experimental import pallas as pl
from jax.experimental.pallas import tpu as pltpu
from jax.sharding import Mesh, PartitionSpec as P

H = 64
KVH = 4
HD = 128
GX = ("z", "x", "c")
ZX = ("z", "x")
NT = (((1,), (1,)), ((), ()))
TN = (((0,), (0,)), ((), ()))
F32 = jnp.float32
BF16 = jnp.bfloat16


def exchange(values, axes):
    return lax.all_to_all(values, axes, split_axis=0, concat_axis=0, tiled=True)


def swap(values, axis, bit):
    n = lax.axis_size(axis)
    return lax.ppermute(values, axis, [(i, i ^ bit) for i in range(n)])


def iota(shape, dim):
    return lax.broadcasted_iota(jnp.int32, shape, dim)


def call(body, outs, ins, flops, size, scratch=()):
    vmem = pl.BlockSpec(memory_space=pltpu.VMEM)
    return pl.pallas_call(
        body,
        out_shape=outs,
        in_specs=[pl.BlockSpec(memory_space=pltpu.SMEM)] + [vmem] * (len(ins) - 1),
        out_specs=jax.tree.map(lambda _: vmem, outs),
        cost_estimate=pl.CostEstimate(flops=flops, bytes_accessed=size, transcendentals=0),
        scratch_shapes=scratch,
    )(*ins)


def pack_body(where, kept, ids, gates, d_out, keys, values, message, kv, ranks):
    top, rows = ids.shape
    slots = message.shape[0]
    tok_dev, width = d_out.shape
    cap = 8
    head = pl.multiple_of(where[0] * HD, HD)
    slot = iota((slots, rows), 0)
    expert = slot // cap
    place = (slot % cap).astype(F32)
    named = jnp.zeros((slots, rows), F32)
    weight = jnp.zeros((slots, rows), F32)
    for j in range(top):
        hit = ids[j : j + 1, :] == expert
        named = jnp.where(hit, 1.0, named)
        weight = jnp.where(hit, gates[j : j + 1, :].astype(F32), weight)
    before = jnp.where(iota((rows, rows), 0) < iota((rows, rows), 1), 1.0, 0.0).astype(BF16)
    rank = jnp.dot(named.astype(BF16), before, preferred_element_type=F32)
    taken = jnp.where((named > 0.0) & (rank == place), 1.0, 0.0)
    pick = jnp.where(kept[...] % tok_dev == iota((tok_dev, rows), 0), 1.0, 0.0).astype(BF16)
    picked = lax.dot_general(pick, d_out[...], TN, preferred_element_type=F32).astype(BF16)
    message[:, :width] = jnp.dot(
        taken.astype(BF16), picked, preferred_element_type=F32
    ).astype(BF16)
    message[:, width:] = jnp.dot(
        (taken * weight).astype(BF16), jnp.ones((rows, HD), BF16), preferred_element_type=F32
    ).astype(BF16)
    for at, source in ((0, keys), (HD, values)):
        kv[:, at : at + HD] = source[:, pl.ds(head, HD)]
    for j in range(top):
        mine = jnp.where((ids[j : j + 1, :] == expert) & (taken > 0.0), place, 0.0)
        ranks[j : j + 1, :] = jnp.sum(mine, axis=0, keepdims=True).astype(jnp.int32)


def attention_body(where, query, grad, mine_in, other_in, d_query, keep, send, mine, other):
    core, block = where[0], where[1]
    keep_dev = query.shape[0]
    heads = query.shape[1] // HD
    rows = keep_dev * heads
    half = mine.shape[0]
    scale = HD ** (-0.5)
    chips = half // keep_dev
    for k in range(chips):
        flip = (k % 8) * 4 + k // 8
        to = pl.ds(pl.multiple_of((block // 2 ^ flip) * keep_dev, keep_dev), keep_dev)
        mine[to, :] = mine_in[k * keep_dev : (k + 1) * keep_dev]
        other[to, :] = other_in[k * keep_dev : (k + 1) * keep_dev]

    def stacked(ref):
        return jnp.concatenate([ref[:, g * HD : (g + 1) * HD] for g in range(heads)], axis=0)

    q = stacked(query)
    o = stacked(grad)
    query_pos = block * keep_dev + iota((rows, half), 0) % keep_dev
    column = iota((rows, half), 1)
    base = column // keep_dev * (2 * keep_dev) + column % keep_dev
    scores = []
    for ref, owner in ((mine, core), (other, 1 - core)):
        s = lax.dot_general(q, ref[:, :HD], NT, preferred_element_type=F32) * scale
        scores.append(jnp.where(base + owner * keep_dev <= query_pos, s, -1e30))
    top = jnp.maximum(*[jnp.max(s, axis=1, keepdims=True) for s in scores])
    expo = [jnp.exp(s - top) for s in scores]
    inv = 1.0 / sum(jnp.sum(e, axis=1, keepdims=True) for e in expo)
    probs = [e * inv for e in expo]
    dps = [
        lax.dot_general(o, ref[:, HD:], NT, preferred_element_type=F32) for ref in (mine, other)
    ]
    mean = sum(jnp.sum(p * dp, axis=1, keepdims=True) for p, dp in zip(probs, dps))
    dq = jnp.zeros((rows, HD), F32)
    for ref, p, dp, out in zip((other, mine), probs[::-1], dps[::-1], (send, keep)):
        ds = (p * (dp - mean)).astype(BF16)
        dk = lax.dot_general(ds, q, TN, preferred_element_type=F32) * scale
        dv = lax.dot_general(p.astype(BF16), o, TN, preferred_element_type=F32)
        out[:, :HD] = dk.astype(BF16)
        out[:, HD:] = dv.astype(BF16)
        dq = dq + jnp.dot(ds, ref[:, :HD], preferred_element_type=F32)
    dq = (dq * scale).astype(BF16)
    for g in range(heads):
        d_query[:, g * HD : (g + 1) * HD] = dq[g * keep_dev : (g + 1) * keep_dev]


def expert_body(weight, rows, gate_pre, up_pre, slot_gate, d_gate, d_up, weighted, dots):
    z = lax.dot_general(weight[...], rows[...], NT, preferred_element_type=F32)
    g = gate_pre[...].astype(F32)
    u = up_pre[...].astype(F32)
    sig = 1.0 / (1.0 + jnp.exp(-g))
    act = g * sig
    hidden = act * u
    one = jnp.where(iota((8, HD), 1) == 0, 1.0, 0.0).astype(BF16)
    scale = lax.dot_general(one, slot_gate[...], NT, preferred_element_type=F32)[0:1]
    grad_hidden = z * scale
    d_up[...] = (grad_hidden * act).astype(BF16)
    d_gate[...] = (grad_hidden * u * sig * (1.0 + g * (1.0 - sig))).astype(BF16)
    weighted[...] = (hidden * scale).astype(BF16)
    blocks, _, lanes = dots.shape
    cap = z.shape[1] // blocks
    spread = jnp.where(
        iota((blocks, lanes), 1) // cap == iota((blocks, lanes), 0),
        jnp.sum(hidden * z, axis=0, keepdims=True),
        0.0,
    )
    place = jnp.where(iota((lanes, lanes), 0) % cap == iota((lanes, lanes), 1), 1.0, 0.0)
    dots[...] = jnp.dot(
        spread, place, preferred_element_type=F32, precision=lax.Precision.HIGHEST
    )[:, None, :]


def down_body(weighted, rows, out):
    out[...] = jnp.dot(weighted[...], rows[...], preferred_element_type=F32).astype(BF16)


def gates_body(where, ids, ranks, returned, out):
    top, rows = ids.shape
    experts = returned.shape[0]
    table = returned[...].reshape(experts, HD)
    result = jnp.zeros((top, HD), F32)
    for j in range(top):
        pick = jnp.where(
            jnp.concatenate([ids[j : j + 1, :]] * (HD // rows), axis=1) == iota((experts, HD), 0),
            1.0,
            0.0,
        )
        found = lax.dot_general(
            table, pick, TN, preferred_element_type=F32, precision=lax.Precision.HIGHEST
        )
        rank = jnp.concatenate([ranks[j : j + 1, :]] * (HD // rows), axis=1)
        hit = jnp.where(iota((HD, HD), 0) == rank, found, 0.0)
        result = jnp.where(iota((top, HD), 0) == j, jnp.sum(hit, axis=0, keepdims=True), result)
    for i in range(out.shape[0]):
        out[i] = result


def total_body(where, terms, out):
    out[...] = jnp.sum(terms[...], axis=0)[:, : out.shape[1]]


def heads_body(where, terms, d_key, d_value):
    keep_dev = d_key.shape[0]
    per = terms.shape[0] // KVH
    for h in range(KVH):
        both = sum(terms[h * per + i, :keep_dev].astype(F32) for i in range(per))
        d_key[:, h * HD : (h + 1) * HD] = both[:, :HD]
        d_value[:, h * HD : (h + 1) * HD] = both[:, HD:]


def on_device(
    d_out, kept, expert_ids, gates, down_weight, gate_pre, up_pre, query, keys, values, d_attn
):
    core = lax.axis_index("c")
    chips = lax.axis_size(ZX)
    me = lax.axis_index("ta")
    n_experts = lax.axis_size(GX)
    n_ta = lax.axis_size("ta")
    keep_dev = kept.shape[0]
    width = d_out.shape[1]
    top = expert_ids.shape[1]
    slots = gate_pre.shape[2]
    cap = slots // n_experts
    hidden = gate_pre.shape[1]
    struct = jax.ShapeDtypeStruct
    ids = expert_ids.T

    local_heads = query.shape[1] // HD
    first_kv = (me * local_heads // (H // KVH)).astype(jnp.int32)
    where = jnp.stack([first_kv, core.astype(jnp.int32), lax.axis_index(GX).astype(jnp.int32)])
    message, kv, ranks = call(
        pack_body,
        (
            struct((slots, width + HD), BF16),
            struct((keep_dev, 2 * HD), BF16),
            struct((top, keep_dev), jnp.int32),
        ),
        (where, kept.reshape(1, keep_dev), ids, gates.T, d_out, keys, values),
        200_000_000,
        3_000_000,
    )
    arrived = exchange(message.reshape(n_experts, cap, -1), GX)
    arrived = arrived.reshape(slots, -1)
    slot_rows = lax.all_gather(arrived[:, :width], "ta", axis=1, tiled=True)
    slot_gate = arrived[:, width:]

    kv_mine = kv
    for axis, bits in (("z", (1, 2, 4)), ("x", (1, 2))):
        for bit in bits:
            got = swap(kv_mine, axis, bit)
            kv_mine = lax.optimization_barrier(jnp.concatenate([kv_mine, got], axis=0))
    kv_other = swap(kv_mine, "c", 1)
    half = chips * keep_dev
    d_query, keep, send = call(
        attention_body,
        (
            struct((keep_dev, local_heads * HD), BF16),
            struct((half, 2 * HD), BF16),
            struct((half, 2 * HD), BF16),
        ),
        (where[1:], query, d_attn, kv_mine, kv_other),
        1_000_000_000,
        4_000_000,
        [pltpu.VMEM((half, 2 * HD), BF16)] * 2,
    )
    chip_part = (keep.astype(F32) + swap(send, "c", 1).astype(F32)).astype(BF16)
    summed = exchange(chip_part.reshape(chips, keep_dev, 2 * HD), ZX)
    owned = jnp.sum(summed.astype(F32), axis=0).astype(BF16)

    copies = exchange(jnp.broadcast_to(owned[None], (n_ta,) + owned.shape), "ta")
    d_key, d_value = call(
        heads_body,
        (struct((keep_dev, KVH * HD), F32), struct((keep_dev, KVH * HD), F32)),
        (where, copies),
        1_000_000,
        1_000_000,
    )

    steps = 4
    some = slots // steps
    few = pl.BlockSpec((hidden, some), lambda i: (0, i))
    blocks = n_experts // steps
    d_gate, d_up, weighted, dots = pl.pallas_call(
        expert_body,
        grid=(steps,),
        in_specs=[
            pl.BlockSpec((hidden, n_ta * width), lambda i: (0, 0)),
            pl.BlockSpec((some, n_ta * width), lambda i: (i, 0)),
            few,
            few,
            pl.BlockSpec((some, HD), lambda i: (i, 0)),
        ],
        out_specs=[few, few, few, pl.BlockSpec((blocks, 1, HD), lambda i: (i, 0, 0))],
        out_shape=[struct((hidden, slots), BF16)] * 3 + [struct((n_experts, 1, HD), F32)],
        cost_estimate=pl.CostEstimate(
            flops=1_000_000_000, bytes_accessed=7_000_000, transcendentals=0
        ),
        name="expert",
    )(down_weight[0], slot_rows, gate_pre[0], up_pre[0], slot_gate)
    columns = n_ta * width // steps
    d_down = pl.pallas_call(
        down_body,
        grid=(steps,),
        in_specs=[
            pl.BlockSpec((hidden, slots), lambda i: (0, 0)),
            pl.BlockSpec((slots, columns), lambda i: (0, i)),
        ],
        out_specs=pl.BlockSpec((hidden, columns), lambda i: (0, i)),
        out_shape=struct(down_weight.shape[1:], BF16),
        cost_estimate=pl.CostEstimate(
            flops=1_000_000_000, bytes_accessed=6_000_000, transcendentals=0
        ),
        name="down",
    )(weighted, slot_rows)
    returned = exchange(dots, GX)
    terms = call(
        gates_body, struct((n_ta, top, HD), F32), (where, ids, ranks, returned), 1_000_000, 100_000
    )
    d_gates = call(
        total_body, struct((top, keep_dev), F32), (where, exchange(terms, "ta")), 100_000, 100_000
    ).T
    return (d_down[None], d_gate[None], d_up[None], d_gates, d_query, d_key, d_value)


def solution(mesh):
    shape = dict(mesh.shape)
    fine = Mesh(mesh.devices.reshape(8, shape["gx"] // 16, 2, shape["ta"]), GX + ("ta",))
    in_specs = (
        P(GX, "ta"),
        P(GX),
        P(GX, None),
        P(GX, None),
        P(GX, "ta", None),
        P(GX, "ta", None),
        P(GX, "ta", None),
        P(GX, "ta"),
        P(GX, None),
        P(GX, None),
        P(GX, "ta"),
    )
    out_specs = (
        P(GX, "ta", None),
        P(GX, "ta", None),
        P(GX, "ta", None),
        P(GX, None),
        P(GX, "ta"),
        P(GX, None),
        P(GX, None),
    )
    return jax.shard_map(
        on_device, mesh=fine, in_specs=in_specs, out_specs=out_specs, check_vma=False
    )
```

```python
import jax
import jax.numpy as jnp
from jax import lax
from jax.experimental import pallas as pl
from jax.experimental.pallas import tpu as pltpu
from jax.sharding import Mesh, PartitionSpec as P

H = 64
KVH = 4
HD = 128
GX = ("z", "x", "c")
ZX = ("z", "x")
NT = (((1,), (1,)), ((), ()))
TN = (((0,), (0,)), ((), ()))
F32 = jnp.float32
BF16 = jnp.bfloat16


def exchange(values, axes):
    return lax.all_to_all(values, axes, split_axis=0, concat_axis=0, tiled=True)


def to_partner(values):
    return lax.ppermute(values, "c", [(0, 1), (1, 0)])


def iota(shape, dim):
    return lax.broadcasted_iota(jnp.int32, shape, dim)


def call(body, outs, ins, flops, size):
    vmem = pl.BlockSpec(memory_space=pltpu.VMEM)
    return pl.pallas_call(
        body,
        out_shape=outs,
        in_specs=[pl.BlockSpec(memory_space=pltpu.SMEM)] + [vmem] * (len(ins) - 1),
        out_specs=jax.tree.map(lambda _: vmem, outs),
        cost_estimate=pl.CostEstimate(flops=flops, bytes_accessed=size, transcendentals=0),
    )(*ins)


def pack_body(where, kept, ids, gates, d_out, keys, values, message, kv, ranks):
    top, rows = ids.shape
    slots = message.shape[0]
    tok_dev, width = d_out.shape
    chips = kv.shape[0] // rows
    cap = 8
    head = pl.multiple_of(where[0] * HD, HD)
    slot = iota((slots, rows), 0)
    expert = slot // cap
    place = (slot % cap).astype(F32)
    named = jnp.zeros((slots, rows), F32)
    weight = jnp.zeros((slots, rows), F32)
    for j in range(top):
        hit = ids[j : j + 1, :] == expert
        named = jnp.where(hit, 1.0, named)
        weight = jnp.where(hit, gates[j : j + 1, :].astype(F32), weight)
    before = jnp.where(iota((rows, rows), 0) < iota((rows, rows), 1), 1.0, 0.0).astype(BF16)
    rank = jnp.dot(named.astype(BF16), before, preferred_element_type=F32)
    taken = jnp.where((named > 0.0) & (rank == place), 1.0, 0.0)
    pick = jnp.where(kept[...] % tok_dev == iota((tok_dev, rows), 0), 1.0, 0.0).astype(BF16)
    picked = lax.dot_general(pick, d_out[...], TN, preferred_element_type=F32).astype(BF16)
    message[:, :width] = jnp.dot(
        taken.astype(BF16), picked, preferred_element_type=F32
    ).astype(BF16)
    message[:, width:] = jnp.dot(
        (taken * weight).astype(BF16), jnp.ones((rows, HD), BF16), preferred_element_type=F32
    ).astype(BF16)
    for at, source in ((0, keys), (HD, values)):
        kv[:, at : at + HD] = jnp.broadcast_to(
            source[:, pl.ds(head, HD)][None], (chips, rows, HD)
        ).reshape(chips * rows, HD)
    for j in range(top):
        mine = jnp.where((ids[j : j + 1, :] == expert) & (taken > 0.0), place, 0.0)
        ranks[j : j + 1, :] = jnp.sum(mine, axis=0, keepdims=True).astype(jnp.int32)


def attention_body(where, query, grad, mine, other, d_query, keep, send):
    core, block = where[0], where[1]
    keep_dev = query.shape[0]
    heads = query.shape[1] // HD
    rows = keep_dev * heads
    half = mine.shape[0]
    scale = HD ** (-0.5)

    def stacked(ref):
        return jnp.concatenate([ref[:, g * HD : (g + 1) * HD] for g in range(heads)], axis=0)

    q = stacked(query)
    o = stacked(grad)
    query_pos = block * keep_dev + iota((rows, half), 0) % keep_dev
    column = iota((rows, half), 1)
    base = column // keep_dev * (2 * keep_dev) + column % keep_dev
    scores = []
    for ref, owner in ((mine, core), (other, 1 - core)):
        s = lax.dot_general(q, ref[:, :HD], NT, preferred_element_type=F32) * scale
        scores.append(jnp.where(base + owner * keep_dev <= query_pos, s, -1e30))
    top = jnp.maximum(*[jnp.max(s, axis=1, keepdims=True) for s in scores])
    expo = [jnp.exp(s - top) for s in scores]
    inv = 1.0 / sum(jnp.sum(e, axis=1, keepdims=True) for e in expo)
    probs = [e * inv for e in expo]
    dps = [
        lax.dot_general(o, ref[:, HD:], NT, preferred_element_type=F32) for ref in (mine, other)
    ]
    mean = sum(jnp.sum(p * dp, axis=1, keepdims=True) for p, dp in zip(probs, dps))
    dq = jnp.zeros((rows, HD), F32)
    for ref, p, dp, out in zip((other, mine), probs[::-1], dps[::-1], (send, keep)):
        ds = (p * (dp - mean)).astype(BF16)
        dk = lax.dot_general(ds, q, TN, preferred_element_type=F32) * scale
        dv = lax.dot_general(p.astype(BF16), o, TN, preferred_element_type=F32)
        out[:, :HD] = dk.astype(BF16)
        out[:, HD:] = dv.astype(BF16)
        dq = dq + jnp.dot(ds, ref[:, :HD], preferred_element_type=F32)
    dq = (dq * scale).astype(BF16)
    for g in range(heads):
        d_query[:, g * HD : (g + 1) * HD] = dq[g * keep_dev : (g + 1) * keep_dev]


def gates_body(where, ids, ranks, returned, owned, out):
    top, rows = ids.shape
    experts = returned.shape[0]
    keep_dev = owned.shape[0]
    table = returned[...].reshape(experts, returned.shape[2])
    result = jnp.zeros((top, HD), F32)
    for j in range(top):
        expert = jnp.concatenate([ids[j : j + 1, :]] * (HD // rows), axis=1)
        rank = jnp.concatenate([ranks[j : j + 1, :]] * (HD // rows), axis=1)
        pick = jnp.where(expert == iota((experts, HD), 0), 1.0, 0.0)
        found = lax.dot_general(
            table, pick, TN, preferred_element_type=F32, precision=lax.Precision.HIGHEST
        )
        hit = jnp.where(iota(found.shape, 0) == rank, found, 0.0)
        result = jnp.where(iota((top, HD), 0) == j, jnp.sum(hit, axis=0, keepdims=True), result)
    high = result.astype(BF16)
    low = (result - high.astype(F32)).astype(BF16)
    for i in range(out.shape[0]):
        out[i, :keep_dev] = owned[...]
        out[i, keep_dev:, :HD] = high
        out[i, keep_dev:, HD:] = low


def final_body(where, terms, d_key, d_value, d_gates):
    keep_dev = d_key.shape[0]
    per = terms.shape[0] // KVH
    for h in range(KVH):
        both = sum(terms[h * per + i, :keep_dev].astype(F32) for i in range(per))
        d_key[:, h * HD : (h + 1) * HD] = both[:, :HD]
        d_value[:, h * HD : (h + 1) * HD] = both[:, HD:]
    parts = jnp.sum(terms[:, keep_dev:, :].astype(F32), axis=0)
    d_gates[...] = (parts[:, :HD] + parts[:, HD:])[:, : d_gates.shape[1]]


def on_device(
    d_out, kept, expert_ids, gates, down_weight, gate_pre, up_pre, query, keys, values, d_attn
):
    core = lax.axis_index("c")
    chips = lax.axis_size(ZX)
    me = lax.axis_index("ta")
    n_experts = lax.axis_size(GX)
    n_ta = lax.axis_size("ta")
    keep_dev = kept.shape[0]
    width = d_out.shape[1]
    top = expert_ids.shape[1]
    slots = gate_pre.shape[2]
    cap = slots // n_experts
    struct = jax.ShapeDtypeStruct
    ids = expert_ids.T

    local_heads = query.shape[1] // HD
    first_kv = (me * local_heads // (H // KVH)).astype(jnp.int32)
    where = jnp.stack([first_kv, core.astype(jnp.int32), lax.axis_index(GX).astype(jnp.int32)])
    message, kv, ranks = call(
        pack_body,
        (
            struct((slots, width + HD), BF16),
            struct((chips * keep_dev, 2 * HD), BF16),
            struct((top, keep_dev), jnp.int32),
        ),
        (where, kept.reshape(1, keep_dev), ids, gates.T, d_out, keys, values),
        200_000_000,
        3_000_000,
    )
    arrived = exchange(message.reshape(n_experts, cap, -1), GX).reshape(slots, -1)
    slot_rows = lax.all_gather(arrived[:, :width], "ta", axis=1, tiled=True)
    slot_gate = arrived[:, width].astype(F32)

    kv_mine = exchange(kv.reshape(chips, keep_dev, 2 * HD), ZX).reshape(-1, 2 * HD)
    kv_other = to_partner(kv_mine)
    half = chips * keep_dev
    d_query, keep, send = call(
        attention_body,
        (
            struct((keep_dev, local_heads * HD), BF16),
            struct((half, 2 * HD), BF16),
            struct((half, 2 * HD), BF16),
        ),
        (where[1:], query, d_attn, kv_mine, kv_other),
        1_000_000_000,
        4_000_000,
    )
    chip_part = (keep.astype(F32) + to_partner(send).astype(F32)).astype(BF16)
    summed = exchange(chip_part.reshape(chips, keep_dev, 2 * HD), ZX)
    owned = jnp.sum(summed.astype(F32), axis=0).astype(BF16)

    z = lax.dot_general(down_weight[0], slot_rows, NT, preferred_element_type=F32)
    g = gate_pre[0].astype(F32)
    u = up_pre[0].astype(F32)
    sig = jax.nn.sigmoid(g)
    act = g * sig
    mixed = act * u
    dots = jnp.sum(mixed * z, axis=0)
    grad_hidden = z * slot_gate[None, :]
    d_up = (grad_hidden * act).astype(BF16)
    d_gate = (grad_hidden * u * sig * (1.0 + g * (1.0 - sig))).astype(BF16)
    weighted = (mixed * slot_gate[None, :]).astype(BF16)
    d_down = jnp.dot(weighted, slot_rows, preferred_element_type=F32).astype(BF16)
    returned = exchange(dots.reshape(n_experts, 1, cap), GX)
    merged = call(
        gates_body,
        struct((n_ta, keep_dev + top, 2 * HD), BF16),
        (where, ids, ranks, returned, owned),
        1_000_000,
        200_000,
    )
    d_key, d_value, d_gates = call(
        final_body,
        (
            struct((keep_dev, KVH * HD), F32),
            struct((keep_dev, KVH * HD), F32),
            struct((top, keep_dev), F32),
        ),
        (where, exchange(merged, "ta")),
        1_000_000,
        300_000,
    )
    return (d_down[None], d_gate[None], d_up[None], d_gates.T, d_query, d_key, d_value)


def solution(mesh):
    shape = dict(mesh.shape)
    fine = Mesh(mesh.devices.reshape(8, shape["gx"] // 16, 2, shape["ta"]), GX + ("ta",))
    in_specs = (
        P(GX, "ta"),
        P(GX),
        P(GX, None),
        P(GX, None),
        P(GX, "ta", None),
        P(GX, "ta", None),
        P(GX, "ta", None),
        P(GX, "ta"),
        P(GX, None),
        P(GX, None),
        P(GX, "ta"),
    )
    out_specs = (
        P(GX, "ta", None),
        P(GX, "ta", None),
        P(GX, "ta", None),
        P(GX, None),
        P(GX, "ta"),
        P(GX, None),
        P(GX, None),
    )
    return jax.shard_map(
        on_device, mesh=fine, in_specs=in_specs, out_specs=out_specs, check_vma=False
    )
```

```python
import jax
import jax.numpy as jnp
from jax import lax
from jax.experimental import pallas as pl
from jax.experimental.pallas import tpu as pltpu
from jax.sharding import Mesh, PartitionSpec as P

H = 64
KVH = 4
HD = 128
GX = ("z", "x", "c")
ZX = ("z", "x")
NT = (((1,), (1,)), ((), ()))
TN = (((0,), (0,)), ((), ()))
F32 = jnp.float32
BF16 = jnp.bfloat16


def exchange(values, axes):
    return lax.all_to_all(values, axes, split_axis=0, concat_axis=0, tiled=True)


def to_partner(values):
    return lax.ppermute(values, "c", [(0, 1), (1, 0)])


def iota(shape, dim):
    return lax.broadcasted_iota(jnp.int32, shape, dim)


def call(body, outs, ins, flops, size):
    vmem = pl.BlockSpec(memory_space=pltpu.VMEM)
    return pl.pallas_call(
        body,
        out_shape=outs,
        in_specs=[pl.BlockSpec(memory_space=pltpu.SMEM)] + [vmem] * (len(ins) - 1),
        out_specs=jax.tree.map(lambda _: vmem, outs),
        cost_estimate=pl.CostEstimate(flops=flops, bytes_accessed=size, transcendentals=0),
    )(*ins)


def named_slots(ids, slots):
    top, rows = ids.shape
    slot = iota((slots, rows), 0)
    expert = slot // 8
    place = (slot % 8).astype(F32)
    named = jnp.zeros((slots, rows), F32)
    for j in range(top):
        named = jnp.where(ids[j : j + 1, :] == expert, 1.0, named)
    before = jnp.where(iota((rows, rows), 0) < iota((rows, rows), 1), 1.0, 0.0).astype(BF16)
    rank = jnp.dot(named.astype(BF16), before, preferred_element_type=F32)
    return jnp.where((named > 0.0) & (rank == place), 1.0, 0.0), expert, place


def pack_body(where, kept, ids, d_out, message):
    rows = ids.shape[1]
    tok_dev = d_out.shape[0]
    taken, _, _ = named_slots(ids, message.shape[0])
    pick = jnp.where(kept[...] % tok_dev == iota((tok_dev, rows), 0), 1.0, 0.0).astype(BF16)
    picked = lax.dot_general(pick, d_out[...], TN, preferred_element_type=F32).astype(BF16)
    message[...] = jnp.dot(taken.astype(BF16), picked, preferred_element_type=F32).astype(BF16)


def tables_body(where, ids, gates, keys, values, kv, ranks, table):
    top, rows = ids.shape
    experts = table.shape[0]
    chips = kv.shape[0] // rows
    head = pl.multiple_of(where[0] * HD, HD)
    for at, source in ((0, keys), (HD, values)):
        kv[:, at : at + HD] = jnp.broadcast_to(
            source[:, pl.ds(head, HD)][None], (chips, rows, HD)
        ).reshape(chips * rows, HD)
    taken, expert, place = named_slots(ids, experts * 8)
    weight = jnp.zeros(taken.shape, F32)
    for j in range(top):
        hit = (ids[j : j + 1, :] == expert) & (taken > 0.0)
        weight = jnp.where(hit, gates[j : j + 1, :].astype(F32), weight)
        ranks[j : j + 1, :] = jnp.sum(
            jnp.where(hit, place, 0.0), axis=0, keepdims=True
        ).astype(jnp.int32)
    column = jnp.dot(weight.astype(BF16), jnp.ones((rows, HD), BF16), preferred_element_type=F32)
    own = jnp.where(iota(column.shape, 0) % 8 == iota(column.shape, 1), column, 0.0)
    table[...] = jnp.sum(own.reshape(experts, 8, HD), axis=1)


def attention_body(where, query, grad, mine, other, d_query, keep, send):
    core, block = where[1], where[2]
    keep_dev = query.shape[0]
    heads = query.shape[1] // HD
    rows = keep_dev * heads
    half = mine.shape[0]
    scale = HD ** (-0.5)

    def stacked(ref):
        return jnp.concatenate([ref[:, g * HD : (g + 1) * HD] for g in range(heads)], axis=0)

    q = stacked(query)
    o = stacked(grad)
    query_pos = block * keep_dev + iota((rows, half), 0) % keep_dev
    column = iota((rows, half), 1)
    base = column // keep_dev * (2 * keep_dev) + column % keep_dev
    scores = []
    for ref, owner in ((mine, core), (other, 1 - core)):
        s = lax.dot_general(q, ref[:, :HD], NT, preferred_element_type=F32) * scale
        scores.append(jnp.where(base + owner * keep_dev <= query_pos, s, -1e30))
    top = jnp.maximum(*[jnp.max(s, axis=1, keepdims=True) for s in scores])
    expo = [jnp.exp(s - top) for s in scores]
    inv = 1.0 / sum(jnp.sum(e, axis=1, keepdims=True) for e in expo)
    probs = [e * inv for e in expo]
    dps = [
        lax.dot_general(o, ref[:, HD:], NT, preferred_element_type=F32) for ref in (mine, other)
    ]
    mean = sum(jnp.sum(p * dp, axis=1, keepdims=True) for p, dp in zip(probs, dps))
    dq = jnp.zeros((rows, HD), F32)
    for ref, p, dp, out in zip((other, mine), probs[::-1], dps[::-1], (send, keep)):
        ds = (p * (dp - mean)).astype(BF16)
        dk = lax.dot_general(ds, q, TN, preferred_element_type=F32) * scale
        dv = lax.dot_general(p.astype(BF16), o, TN, preferred_element_type=F32)
        out[:, :HD] = dk.astype(BF16)
        out[:, HD:] = dv.astype(BF16)
        dq = dq + jnp.dot(ds, ref[:, :HD], preferred_element_type=F32)
    dq = (dq * scale).astype(BF16)
    for g in range(heads):
        d_query[:, g * HD : (g + 1) * HD] = dq[g * keep_dev : (g + 1) * keep_dev]


def gates_body(where, ids, ranks, returned, owned, out):
    top, rows = ids.shape
    experts = returned.shape[0]
    keep_dev = owned.shape[0]
    table = returned[...].reshape(experts, returned.shape[2])[:, :8]
    result = jnp.zeros((top, HD), F32)
    for j in range(top):
        expert = jnp.concatenate([ids[j : j + 1, :]] * (HD // rows), axis=1)
        rank = jnp.concatenate([ranks[j : j + 1, :]] * (HD // rows), axis=1)
        pick = jnp.where(expert == iota((experts, HD), 0), 1.0, 0.0)
        found = lax.dot_general(
            table, pick, TN, preferred_element_type=F32, precision=lax.Precision.HIGHEST
        )
        hit = jnp.where(iota(found.shape, 0) == rank, found, 0.0)
        result = jnp.where(iota((top, HD), 0) == j, jnp.sum(hit, axis=0, keepdims=True), result)
    high = result.astype(BF16)
    low = (result - high.astype(F32)).astype(BF16)
    for i in range(out.shape[0]):
        out[i, :keep_dev] = owned[...]
        out[i, keep_dev:, :HD] = high
        out[i, keep_dev:, HD:] = low


def final_body(where, terms, d_key, d_value, d_gates):
    keep_dev = d_key.shape[0]
    per = terms.shape[0] // KVH
    for h in range(KVH):
        both = sum(terms[h * per + i, :keep_dev].astype(F32) for i in range(per))
        d_key[:, h * HD : (h + 1) * HD] = both[:, :HD]
        d_value[:, h * HD : (h + 1) * HD] = both[:, HD:]
    parts = jnp.sum(terms[:, keep_dev:, :].astype(F32), axis=0)
    d_gates[...] = (parts[:, :HD] + parts[:, HD:])[:, : d_gates.shape[1]]


def on_device(
    d_out, kept, expert_ids, gates, down_weight, gate_pre, up_pre, query, keys, values, d_attn
):
    core = lax.axis_index("c")
    chips = lax.axis_size(ZX)
    me = lax.axis_index("ta")
    n_experts = lax.axis_size(GX)
    n_ta = lax.axis_size("ta")
    keep_dev = kept.shape[0]
    width = d_out.shape[1]
    top = expert_ids.shape[1]
    slots = gate_pre.shape[2]
    cap = slots // n_experts
    struct = jax.ShapeDtypeStruct
    ids = expert_ids.T

    local_heads = query.shape[1] // HD
    first_kv = (me * local_heads // (H // KVH)).astype(jnp.int32)
    where = jnp.stack([first_kv, core.astype(jnp.int32), lax.axis_index(GX).astype(jnp.int32)])
    message = call(
        pack_body,
        struct((slots, width), BF16),
        (where, kept.reshape(1, keep_dev), ids, d_out),
        200_000_000,
        2_000_000,
    )
    arrived = exchange(message.reshape(n_experts, cap, width), GX)
    kv, ranks, table = call(
        tables_body,
        (
            struct((chips * keep_dev, 2 * HD), BF16),
            struct((top, keep_dev), jnp.int32),
            struct((n_experts, HD), F32),
        ),
        (where, ids, gates.T, keys, values),
        10_000_000,
        1_000_000,
    )
    slot_rows = lax.all_gather(arrived.reshape(slots, width), "ta", axis=1, tiled=True)

    kv_mine = exchange(kv.reshape(chips, keep_dev, 2 * HD), ZX).reshape(-1, 2 * HD)
    kv_other = to_partner(kv_mine)
    half = chips * keep_dev
    d_query, keep, send = call(
        attention_body,
        (
            struct((keep_dev, local_heads * HD), BF16),
            struct((half, 2 * HD), BF16),
            struct((half, 2 * HD), BF16),
        ),
        (where, query, d_attn, kv_mine, kv_other),
        1_000_000_000,
        4_000_000,
    )
    chip_part = (keep.astype(F32) + to_partner(send).astype(F32)).astype(BF16)
    summed = exchange(chip_part.reshape(chips, keep_dev, 2 * HD), ZX)
    owned = jnp.sum(summed.astype(F32), axis=0).astype(BF16)

    z = lax.dot_general(down_weight[0], slot_rows, NT, preferred_element_type=F32)
    g = gate_pre[0].astype(F32)
    u = up_pre[0].astype(F32)
    sig = jax.nn.sigmoid(g)
    act = g * sig
    mixed = act * u
    dots = jnp.sum(mixed * z, axis=0)
    both = jnp.concatenate(
        [dots.reshape(n_experts, 1, cap), table[:, :cap].reshape(n_experts, 1, cap)], axis=2
    )
    returned = exchange(both, GX)
    slot_weight = returned[:, 0, cap:].reshape(1, slots)
    grad_hidden = z * slot_weight
    d_up = (grad_hidden * act).astype(BF16)
    d_gate = (grad_hidden * u * sig * (1.0 + g * (1.0 - sig))).astype(BF16)
    weighted = (mixed * slot_weight).astype(BF16)
    d_down = jnp.dot(weighted, slot_rows, preferred_element_type=F32).astype(BF16)
    merged = call(
        gates_body,
        struct((n_ta, keep_dev + top, 2 * HD), BF16),
        (where, ids, ranks, returned, owned),
        1_000_000,
        200_000,
    )
    d_key, d_value, d_gates = call(
        final_body,
        (
            struct((keep_dev, KVH * HD), F32),
            struct((keep_dev, KVH * HD), F32),
            struct((top, keep_dev), F32),
        ),
        (where, exchange(merged, "ta")),
        1_000_000,
        300_000,
    )
    return (d_down[None], d_gate[None], d_up[None], d_gates.T, d_query, d_key, d_value)


def solution(mesh):
    shape = dict(mesh.shape)
    fine = Mesh(mesh.devices.reshape(8, shape["gx"] // 16, 2, shape["ta"]), GX + ("ta",))
    in_specs = (
        P(GX, "ta"),
        P(GX),
        P(GX, None),
        P(GX, None),
        P(GX, "ta", None),
        P(GX, "ta", None),
        P(GX, "ta", None),
        P(GX, "ta"),
        P(GX, None),
        P(GX, None),
        P(GX, "ta"),
    )
    out_specs = (
        P(GX, "ta", None),
        P(GX, "ta", None),
        P(GX, "ta", None),
        P(GX, None),
        P(GX, "ta"),
        P(GX, None),
        P(GX, None),
    )
    return jax.shard_map(
        on_device, mesh=fine, in_specs=in_specs, out_specs=out_specs, check_vma=False
    )
```

```python
import jax
import jax.numpy as jnp
from jax import lax
from jax.experimental import pallas as pl
from jax.experimental.pallas import tpu as pltpu
from jax.sharding import Mesh, PartitionSpec as P

H = 64
KVH = 4
HD = 128
GX = ("z", "x", "c")
ZX = ("z", "x")
NT = (((1,), (1,)), ((), ()))
TN = (((0,), (0,)), ((), ()))
F32 = jnp.float32
BF16 = jnp.bfloat16


def exchange(values, axes):
    return lax.all_to_all(values, axes, split_axis=0, concat_axis=0, tiled=True)


def to_partner(values):
    return lax.ppermute(values, "c", [(0, 1), (1, 0)])


def iota(shape, dim):
    return lax.broadcasted_iota(jnp.int32, shape, dim)


def call(body, outs, ins, flops, size, scalars=1, room=None):
    vmem = pl.BlockSpec(memory_space=pltpu.VMEM)
    smem = pl.BlockSpec(memory_space=pltpu.SMEM)
    return pl.pallas_call(
        body,
        out_shape=outs,
        in_specs=[smem] * scalars + [vmem] * (len(ins) - scalars),
        out_specs=jax.tree.map(lambda _: vmem, outs),
        cost_estimate=pl.CostEstimate(flops=flops, bytes_accessed=size, transcendentals=0),
        compiler_params=pltpu.CompilerParams(vmem_limit_bytes=room and room << 20),
    )(*ins)


def named_slots(ids, slots):
    top, rows = ids.shape
    slot = iota((slots, rows), 0)
    expert = slot // 8
    place = (slot % 8).astype(F32)
    named = jnp.zeros((slots, rows), F32)
    for j in range(top):
        named = jnp.where(ids[j : j + 1, :] == expert, 1.0, named)
    before = jnp.where(iota((rows, rows), 0) < iota((rows, rows), 1), 1.0, 0.0).astype(BF16)
    rank = jnp.dot(named.astype(BF16), before, preferred_element_type=F32)
    return jnp.where((named > 0.0) & (rank == place), 1.0, 0.0), expert, place


def pack_body(kept, ids, d_out, message):
    rows = ids.shape[1]
    tok_dev = d_out.shape[0]
    taken, _, _ = named_slots(ids, message.shape[0])
    pick = jnp.where(kept[...] % tok_dev == iota((tok_dev, rows), 0), 1.0, 0.0).astype(BF16)
    picked = lax.dot_general(pick, d_out[...], TN, preferred_element_type=F32).astype(BF16)
    message[...] = jnp.dot(taken.astype(BF16), picked, preferred_element_type=F32).astype(BF16)


def tables_body(where, ids, gates, keys, values, kv, code, table):
    top, rows = ids.shape
    experts = table.shape[0]
    chips = kv.shape[0] // rows
    head = pl.multiple_of(where[0] * HD, HD)
    for at, source in ((0, keys), (HD, values)):
        kv[:, at : at + HD] = jnp.broadcast_to(
            source[:, pl.ds(head, HD)][None], (chips, rows, HD)
        ).reshape(chips * rows, HD)
    taken, expert, place = named_slots(ids, experts * 8)
    weight = jnp.zeros(taken.shape, F32)
    ranks = []
    for j in range(top):
        hit = (ids[j : j + 1, :] == expert) & (taken > 0.0)
        weight = jnp.where(hit, gates[j : j + 1, :].astype(F32), weight)
        ranks.append(
            jnp.sum(jnp.where(hit, place, 0.0), axis=0, keepdims=True).astype(jnp.int32)
        )
    code[0:1, :] = jnp.concatenate([ids[j : j + 1, :] for j in range(top)], axis=1)
    code[1:2, :] = jnp.concatenate(ranks, axis=1)
    column = jnp.dot(weight.astype(BF16), jnp.ones((rows, HD), BF16), preferred_element_type=F32)
    own = jnp.where(iota(column.shape, 0) % 8 == iota(column.shape, 1), column, 0.0)
    table[...] = jnp.sum(own.reshape(experts, 8, HD), axis=1)


def attention_body(where, query, grad, mine, other, d_query, keep, send):
    core, block = where[1], where[2]
    keep_dev = query.shape[0]
    heads = query.shape[1] // HD
    rows = keep_dev * heads
    half = mine.shape[0]
    scale = HD ** (-0.5)

    def stacked(ref):
        return jnp.concatenate([ref[:, g * HD : (g + 1) * HD] for g in range(heads)], axis=0)

    q = stacked(query)
    o = stacked(grad)
    query_pos = block * keep_dev + iota((rows, half), 0) % keep_dev
    column = iota((rows, half), 1)
    base = column // keep_dev * (2 * keep_dev) + column % keep_dev
    scores = []
    for ref, owner in ((mine, core), (other, 1 - core)):
        s = lax.dot_general(q, ref[:, :HD], NT, preferred_element_type=F32) * scale
        scores.append(jnp.where(base + owner * keep_dev <= query_pos, s, -1e30))
    top = jnp.maximum(*[jnp.max(s, axis=1, keepdims=True) for s in scores])
    expo = [jnp.exp(s - top) for s in scores]
    inv = 1.0 / sum(jnp.sum(e, axis=1, keepdims=True) for e in expo)
    probs = [e * inv for e in expo]
    dps = [
        lax.dot_general(o, ref[:, HD:], NT, preferred_element_type=F32) for ref in (mine, other)
    ]
    mean = sum(jnp.sum(p * dp, axis=1, keepdims=True) for p, dp in zip(probs, dps))
    dq = jnp.zeros((rows, HD), F32)
    for ref, p, dp, out in zip((other, mine), probs[::-1], dps[::-1], (send, keep)):
        ds = (p * (dp - mean)).astype(BF16)
        dk = lax.dot_general(ds, q, TN, preferred_element_type=F32) * scale
        dv = lax.dot_general(p.astype(BF16), o, TN, preferred_element_type=F32)
        out[:, :HD] = dk.astype(BF16)
        out[:, HD:] = dv.astype(BF16)
        dq = dq + jnp.dot(ds, ref[:, :HD], preferred_element_type=F32)
    dq = (dq * scale).astype(BF16)
    for g in range(heads):
        d_query[:, g * HD : (g + 1) * HD] = dq[g * keep_dev : (g + 1) * keep_dev]


def gates_body(code, got, owned, out):
    experts = got.shape[0]
    keep_dev = owned.shape[0]
    pairs = code.shape[1]
    pick = jnp.where(code[0:1, :] == iota((experts, pairs), 0), 1.0, 0.0)
    table = got[...].reshape(experts, got.shape[2])[:, :8]
    found = lax.dot_general(
        table, pick, TN, preferred_element_type=F32, precision=lax.Precision.HIGHEST
    )
    hit = jnp.where(iota(found.shape, 0) == code[1:2, :], found, 0.0)
    result = jnp.sum(hit, axis=0, keepdims=True)
    high = result.astype(BF16).astype(F32)
    row = iota((8, pairs), 0)
    tail = jnp.where(row == 0, high, jnp.where(row == 1, result - high, 0.0)).astype(BF16)
    for i in range(out.shape[0]):
        out[i, :keep_dev] = owned[...]
        out[i, keep_dev:] = tail


def final_body(terms, d_key, d_value, d_gates):
    top, keep_dev = d_gates.shape
    per = terms.shape[0] // KVH
    for h in range(KVH):
        both = sum(terms[h * per + i, :keep_dev].astype(F32) for i in range(per))
        d_key[:, h * HD : (h + 1) * HD] = both[:, :HD]
        d_value[:, h * HD : (h + 1) * HD] = both[:, HD:]
    parts = jnp.sum(terms[:, keep_dev:, :].astype(F32), axis=0)
    flat = parts[0:1] + parts[1:2]
    for j in range(top):
        d_gates[j : j + 1, :] = flat[:, j * keep_dev : (j + 1) * keep_dev]


def on_device(
    d_out, kept, expert_ids, gates, down_weight, gate_pre, up_pre, query, keys, values, d_attn
):
    core = lax.axis_index("c")
    chips = lax.axis_size(ZX)
    me = lax.axis_index("ta")
    n_experts = lax.axis_size(GX)
    n_ta = lax.axis_size("ta")
    keep_dev = kept.shape[0]
    width = d_out.shape[1]
    top = expert_ids.shape[1]
    slots = gate_pre.shape[2]
    cap = slots // n_experts
    struct = jax.ShapeDtypeStruct
    ids = expert_ids.T

    local_heads = query.shape[1] // HD
    first_kv = (me * local_heads // (H // KVH)).astype(jnp.int32)
    where = jnp.stack([first_kv, core.astype(jnp.int32), lax.axis_index(GX).astype(jnp.int32)])
    message = call(
        pack_body,
        struct((slots, width), BF16),
        (kept.reshape(1, keep_dev), ids, d_out),
        200_000_000,
        2_000_000,
        scalars=0,
    )
    arrived = exchange(message.reshape(n_experts, cap, width), GX)
    kv, code, table = call(
        tables_body,
        (
            struct((chips * keep_dev, 2 * HD), BF16),
            struct((2, top * keep_dev), jnp.int32),
            struct((n_experts, HD), F32),
        ),
        (where, ids, gates.T, keys, values),
        10_000_000,
        1_000_000,
    )
    slot_rows = lax.all_gather(arrived.reshape(slots, width), "ta", axis=1, tiled=True)

    kv_mine = exchange(kv.reshape(chips, keep_dev, 2 * HD), ZX).reshape(-1, 2 * HD)
    kv_other = to_partner(kv_mine)
    half = chips * keep_dev
    d_query, keep, send = call(
        attention_body,
        (
            struct((keep_dev, local_heads * HD), BF16),
            struct((half, 2 * HD), BF16),
            struct((half, 2 * HD), BF16),
        ),
        (where, query, d_attn, kv_mine, kv_other),
        1_000_000_000,
        4_000_000,
        room=24,
    )
    chip_part = (keep.astype(F32) + to_partner(send).astype(F32)).astype(BF16)
    summed = exchange(chip_part.reshape(chips, keep_dev, 2 * HD), ZX)
    owned = jnp.sum(summed.astype(F32), axis=0).astype(BF16)

    z = lax.dot_general(down_weight[0], slot_rows, NT, preferred_element_type=F32)
    g = gate_pre[0].astype(F32)
    u = up_pre[0].astype(F32)
    sig = jax.nn.sigmoid(g)
    act = g * sig
    mixed = act * u
    dots = jnp.sum(mixed * z, axis=0)
    both = jnp.concatenate(
        [dots.reshape(n_experts, 1, cap), table[:, :cap].reshape(n_experts, 1, cap)], axis=2
    )
    returned = exchange(both, GX)
    slot_weight = returned[:, 0, cap:].reshape(1, slots)
    grad_hidden = z * slot_weight
    d_up = (grad_hidden * act).astype(BF16)
    d_gate = (grad_hidden * u * sig * (1.0 + g * (1.0 - sig))).astype(BF16)
    weighted = (mixed * slot_weight).astype(BF16)
    d_down = jnp.dot(weighted, slot_rows, preferred_element_type=F32).astype(BF16)
    merged = call(
        gates_body,
        struct((n_ta, keep_dev + top, 2 * HD), BF16),
        (code, returned, owned),
        1_000_000,
        200_000,
        scalars=0,
        room=8,
    )
    d_key, d_value, d_gates = call(
        final_body,
        (
            struct((keep_dev, KVH * HD), F32),
            struct((keep_dev, KVH * HD), F32),
            struct((top, keep_dev), F32),
        ),
        (exchange(merged, "ta"),),
        1_000_000,
        300_000,
        scalars=0,
        room=8,
    )
    return (d_down[None], d_gate[None], d_up[None], d_gates.T, d_query, d_key, d_value)


def solution(mesh):
    shape = dict(mesh.shape)
    fine = Mesh(mesh.devices.reshape(8, shape["gx"] // 16, 2, shape["ta"]), GX + ("ta",))
    in_specs = (
        P(GX, "ta"),
        P(GX),
        P(GX, None),
        P(GX, None),
        P(GX, "ta", None),
        P(GX, "ta", None),
        P(GX, "ta", None),
        P(GX, "ta"),
        P(GX, None),
        P(GX, None),
        P(GX, "ta"),
    )
    out_specs = (
        P(GX, "ta", None),
        P(GX, "ta", None),
        P(GX, "ta", None),
        P(GX, None),
        P(GX, "ta"),
        P(GX, None),
        P(GX, None),
    )
    return jax.shard_map(
        on_device, mesh=fine, in_specs=in_specs, out_specs=out_specs, check_vma=False
    )
```

```python
import jax
import jax.numpy as jnp
from jax import lax
from jax.experimental import pallas as pl
from jax.experimental.pallas import tpu as pltpu
from jax.sharding import Mesh, PartitionSpec as P

H = 64
KVH = 4
HD = 128
GX = ("z", "x", "c")
ZX = ("z", "x")
NT = (((1,), (1,)), ((), ()))
TN = (((0,), (0,)), ((), ()))
F32 = jnp.float32
BF16 = jnp.bfloat16


def exchange(values, axes):
    return lax.all_to_all(values, axes, split_axis=0, concat_axis=0, tiled=True)


def to_partner(values):
    return lax.ppermute(values, "c", [(0, 1), (1, 0)])


def iota(shape, dim):
    return lax.broadcasted_iota(jnp.int32, shape, dim)


def call(body, outs, ins, flops, size, scalars=1, room=None):
    vmem = pl.BlockSpec(memory_space=pltpu.VMEM)
    smem = pl.BlockSpec(memory_space=pltpu.SMEM)
    return pl.pallas_call(
        body,
        out_shape=outs,
        in_specs=[smem] * scalars + [vmem] * (len(ins) - scalars),
        out_specs=jax.tree.map(lambda _: vmem, outs),
        cost_estimate=pl.CostEstimate(flops=flops, bytes_accessed=size, transcendentals=0),
        compiler_params=pltpu.CompilerParams(vmem_limit_bytes=room and room << 20),
    )(*ins)


def named_slots(ids, slots):
    top, rows = ids.shape
    slot = iota((slots, rows), 0)
    expert = slot // 8
    place = (slot % 8).astype(F32)
    named = jnp.zeros((slots, rows), F32)
    for j in range(top):
        named = jnp.where(ids[j : j + 1, :] == expert, 1.0, named)
    before = jnp.where(iota((rows, rows), 0) < iota((rows, rows), 1), 1.0, 0.0).astype(BF16)
    rank = jnp.dot(named.astype(BF16), before, preferred_element_type=F32)
    return jnp.where((named > 0.0) & (rank == place), 1.0, 0.0), expert, place


def pack_body(kept, ids, d_out, message):
    rows = ids.shape[1]
    tok_dev = d_out.shape[0]
    taken, _, _ = named_slots(ids, message.shape[0])
    pick = jnp.where(kept[...] % tok_dev == iota((tok_dev, rows), 0), 1.0, 0.0).astype(BF16)
    picked = lax.dot_general(pick, d_out[...], TN, preferred_element_type=F32).astype(BF16)
    message[...] = jnp.dot(taken.astype(BF16), picked, preferred_element_type=F32).astype(BF16)


def tables_body(where, ids, gates, keys, values, query, grad, kv, code, table, q, o):
    top, rows = ids.shape
    experts = table.shape[0]
    chips = kv.shape[0] // rows
    head = pl.multiple_of(where[0] * HD, HD)
    for to, source in ((q, query), (o, grad)):
        for g in range(source.shape[1] // HD):
            to[g * rows : (g + 1) * rows, :] = source[:, g * HD : (g + 1) * HD]
    for at, source in ((0, keys), (HD, values)):
        kv[:, at : at + HD] = jnp.broadcast_to(
            source[:, pl.ds(head, HD)][None], (chips, rows, HD)
        ).reshape(chips * rows, HD)
    taken, expert, place = named_slots(ids, experts * 8)
    weight = jnp.zeros(taken.shape, F32)
    ranks = []
    for j in range(top):
        hit = (ids[j : j + 1, :] == expert) & (taken > 0.0)
        weight = jnp.where(hit, gates[j : j + 1, :].astype(F32), weight)
        ranks.append(
            jnp.sum(jnp.where(hit, place, 0.0), axis=0, keepdims=True).astype(jnp.int32)
        )
    code[0:1, :] = jnp.concatenate([ids[j : j + 1, :] for j in range(top)], axis=1)
    code[1:2, :] = jnp.concatenate(ranks, axis=1)
    column = jnp.dot(weight.astype(BF16), jnp.ones((rows, HD), BF16), preferred_element_type=F32)
    own = jnp.where(iota(column.shape, 0) % 8 == iota(column.shape, 1), column, 0.0)
    table[...] = jnp.sum(own.reshape(experts, 8, HD), axis=1)


def attention_body(where, query, grad, mine, other, d_query, keep, send):
    core, block = where[1], where[2]
    keep_dev = d_query.shape[0]
    heads = d_query.shape[1] // HD
    rows = keep_dev * heads
    half = mine.shape[0]
    scale = HD ** (-0.5)
    q = query[...]
    o = grad[...]
    query_pos = block * keep_dev + iota((rows, half), 0) % keep_dev
    column = iota((rows, half), 1)
    base = column // keep_dev * (2 * keep_dev) + column % keep_dev
    scores = []
    for ref, owner in ((mine, core), (other, 1 - core)):
        s = lax.dot_general(q, ref[:, :HD], NT, preferred_element_type=F32) * scale
        scores.append(jnp.where(base + owner * keep_dev <= query_pos, s, -1e30))
    top = jnp.maximum(*[jnp.max(s, axis=1, keepdims=True) for s in scores])
    expo = [jnp.exp(s - top) for s in scores]
    inv = 1.0 / sum(jnp.sum(e, axis=1, keepdims=True) for e in expo)
    probs = [e * inv for e in expo]
    dps = [
        lax.dot_general(o, ref[:, HD:], NT, preferred_element_type=F32) for ref in (mine, other)
    ]
    mean = sum(jnp.sum(p * dp, axis=1, keepdims=True) for p, dp in zip(probs, dps))
    dq = jnp.zeros((rows, HD), F32)
    for ref, p, dp, out in zip((other, mine), probs[::-1], dps[::-1], (send, keep)):
        ds = (p * (dp - mean)).astype(BF16)
        dk = lax.dot_general(ds, q, TN, preferred_element_type=F32) * scale
        dv = lax.dot_general(p.astype(BF16), o, TN, preferred_element_type=F32)
        out[:, :HD] = dk.astype(BF16)
        out[:, HD:] = dv.astype(BF16)
        dq = dq + jnp.dot(ds, ref[:, :HD], preferred_element_type=F32)
    dq = (dq * scale).astype(BF16)
    for g in range(heads):
        d_query[:, g * HD : (g + 1) * HD] = dq[g * keep_dev : (g + 1) * keep_dev]


def gates_body(code, got, owned, out):
    experts = got.shape[0]
    keep_dev = owned.shape[0]
    pairs = code.shape[1]
    pick = jnp.where(code[0:1, :] == iota((experts, pairs), 0), 1.0, 0.0)
    table = got[...].reshape(experts, got.shape[2])[:, :8]
    found = lax.dot_general(
        table, pick, TN, preferred_element_type=F32, precision=lax.Precision.HIGHEST
    )
    hit = jnp.where(iota(found.shape, 0) == code[1:2, :], found, 0.0)
    result = jnp.sum(hit, axis=0, keepdims=True)
    high = result.astype(BF16).astype(F32)
    row = iota((8, pairs), 0)
    tail = jnp.where(row == 0, high, jnp.where(row == 1, result - high, 0.0)).astype(BF16)
    for i in range(out.shape[0]):
        out[i, :keep_dev] = owned[...]
        out[i, keep_dev:] = tail


def final_body(terms, d_key, d_value, d_gates):
    top, keep_dev = d_gates.shape
    per = terms.shape[0] // KVH
    for h in range(KVH):
        both = sum(terms[h * per + i, :keep_dev].astype(F32) for i in range(per))
        d_key[:, h * HD : (h + 1) * HD] = both[:, :HD]
        d_value[:, h * HD : (h + 1) * HD] = both[:, HD:]
    parts = jnp.sum(terms[:, keep_dev:, :].astype(F32), axis=0)
    flat = parts[0:1] + parts[1:2]
    for j in range(top):
        d_gates[j : j + 1, :] = flat[:, j * keep_dev : (j + 1) * keep_dev]


def on_device(
    d_out, kept, expert_ids, gates, down_weight, gate_pre, up_pre, query, keys, values, d_attn
):
    core = lax.axis_index("c")
    chips = lax.axis_size(ZX)
    me = lax.axis_index("ta")
    n_experts = lax.axis_size(GX)
    n_ta = lax.axis_size("ta")
    keep_dev = kept.shape[0]
    width = d_out.shape[1]
    top = expert_ids.shape[1]
    slots = gate_pre.shape[2]
    cap = slots // n_experts
    struct = jax.ShapeDtypeStruct
    ids = expert_ids.T

    local_heads = query.shape[1] // HD
    first_kv = (me * local_heads // (H // KVH)).astype(jnp.int32)
    where = jnp.stack([first_kv, core.astype(jnp.int32), lax.axis_index(GX).astype(jnp.int32)])
    message = call(
        pack_body,
        struct((slots, width), BF16),
        (kept.reshape(1, keep_dev), ids, d_out),
        200_000_000,
        2_000_000,
        scalars=0,
    )
    arrived = exchange(message.reshape(n_experts, cap, width), GX)
    kv, code, table, q_rows, o_rows = call(
        tables_body,
        (
            struct((chips * keep_dev, 2 * HD), BF16),
            struct((2, top * keep_dev), jnp.int32),
            struct((n_experts, HD), F32),
            struct((keep_dev * local_heads, HD), BF16),
            struct((keep_dev * local_heads, HD), BF16),
        ),
        (where, ids, gates.T, keys, values, query, d_attn),
        10_000_000,
        1_000_000,
        room=8,
    )
    slot_rows = lax.all_gather(arrived.reshape(slots, width), "ta", axis=1, tiled=True)

    kv_mine = exchange(kv.reshape(chips, keep_dev, 2 * HD), ZX).reshape(-1, 2 * HD)
    kv_other = to_partner(kv_mine)
    half = chips * keep_dev
    d_query, keep, send = call(
        attention_body,
        (
            struct((keep_dev, local_heads * HD), BF16),
            struct((half, 2 * HD), BF16),
            struct((half, 2 * HD), BF16),
        ),
        (where, q_rows, o_rows, kv_mine, kv_other),
        1_000_000_000,
        4_000_000,
        room=24,
    )
    chip_part = (keep.astype(F32) + to_partner(send).astype(F32)).astype(BF16)
    summed = exchange(chip_part.reshape(chips, keep_dev, 2 * HD), ZX)
    owned = jnp.sum(summed.astype(F32), axis=0).astype(BF16)

    z = lax.dot_general(down_weight[0], slot_rows, NT, preferred_element_type=F32)
    g = gate_pre[0].astype(F32)
    u = up_pre[0].astype(F32)
    sig = jax.nn.sigmoid(g)
    act = g * sig
    mixed = act * u
    dots = jnp.sum(mixed * z, axis=0)
    both = jnp.concatenate(
        [dots.reshape(n_experts, 1, cap), table[:, :cap].reshape(n_experts, 1, cap)], axis=2
    )
    returned = exchange(both, GX)
    slot_weight = returned[:, 0, cap:].reshape(1, slots)
    grad_hidden = z * slot_weight
    d_up = (grad_hidden * act).astype(BF16)
    d_gate = (grad_hidden * u * sig * (1.0 + g * (1.0 - sig))).astype(BF16)
    weighted = (mixed * slot_weight).astype(BF16)
    d_down = jnp.dot(weighted, slot_rows, preferred_element_type=F32).astype(BF16)
    merged = call(
        gates_body,
        struct((n_ta, keep_dev + top, 2 * HD), BF16),
        (code, returned, owned),
        1_000_000,
        200_000,
        scalars=0,
        room=8,
    )
    d_key, d_value, d_gates = call(
        final_body,
        (
            struct((keep_dev, KVH * HD), F32),
            struct((keep_dev, KVH * HD), F32),
            struct((top, keep_dev), F32),
        ),
        (exchange(merged, "ta"),),
        1_000_000,
        300_000,
        scalars=0,
        room=8,
    )
    return (d_down[None], d_gate[None], d_up[None], d_gates.T, d_query, d_key, d_value)


def solution(mesh):
    shape = dict(mesh.shape)
    fine = Mesh(mesh.devices.reshape(8, shape["gx"] // 16, 2, shape["ta"]), GX + ("ta",))
    in_specs = (
        P(GX, "ta"),
        P(GX),
        P(GX, None),
        P(GX, None),
        P(GX, "ta", None),
        P(GX, "ta", None),
        P(GX, "ta", None),
        P(GX, "ta"),
        P(GX, None),
        P(GX, None),
        P(GX, "ta"),
    )
    out_specs = (
        P(GX, "ta", None),
        P(GX, "ta", None),
        P(GX, "ta", None),
        P(GX, None),
        P(GX, "ta"),
        P(GX, None),
        P(GX, None),
    )
    return jax.shard_map(
        on_device, mesh=fine, in_specs=in_specs, out_specs=out_specs, check_vma=False
    )
```
